256 devices in a mesh: loop: 4 (over x_lo, core), sub: 64 (over z, y, x_hi).
Axes of the slice: x: 4 (x_hi: 2, x_lo: 2; x = x_hi * 2 + x_lo), y: 4, z: 8, core: 2. Of those that a mesh axis runs over, the one named last changes fastest.
Arguments:
- rate: float32 [8192, 5, 384], P(('loop', 'sub')), may hold values from 0 to 1
- phase: float32 [8192, 5, 384], P(('loop', 'sub')), may hold values from -3.140625 to 3.140625
- forcing: float32 [2, 4, 8192, 5, 384], P(None, None, ('loop', 'sub')), may hold values from -8 to 8
Outputs:
- response: float32 [2, 4, 8192, 5, 384], P(None, None, ('loop', 'sub'))
The draws below stay inside these ranges and needn't reach their ends.
All inputs are finite; a program needn't handle non-finite values.
Results may differ from the reference program's by a relative error of at most 0.0003.
Values sent between devices are 32-bit elements; how exact they have to be, the bound alone decides.
A program may use at most 128 MiB of HBM per device.

```python
import jax
import jax.numpy as jnp
from jax import lax

FIELDS = 5
WALL = 384
EXCITATIONS = 4
STAT_DEV = 32
AXIAL_POSITIONS = 8192


def draw_rate(key, part):
    generator_seeds = jax.random.split(key, 5)
    share = 0.5
    pick = jax.random.uniform(generator_seeds[0], (FIELDS, WALL)) < share
    level = jax.random.uniform(generator_seeds[1], (FIELDS, WALL))
    slow = jnp.exp(jnp.log(0.3 / AXIAL_POSITIONS) + level * jnp.log(5.0))
    fast = 0.02 * jnp.exp(level * jnp.log(1.75))
    mean_velocity_shape = jnp.where(pick, slow, fast)
    stochastic_perturbation = jnp.exp(jax.random.uniform(generator_seeds[2], (AXIAL_POSITIONS, FIELDS, WALL), minval=jnp.log(0.5), maxval=jnp.log(2.0)))
    excitation_pulse = jax.random.bernoulli(generator_seeds[3], 2.0 / AXIAL_POSITIONS, (AXIAL_POSITIONS, 1, 1))
    excitation_strength = jax.random.uniform(generator_seeds[4], (AXIAL_POSITIONS, 1, 1), minval=0.22, maxval=0.69)
    return (mean_velocity_shape[None] * stochastic_perturbation + jnp.where(excitation_pulse, excitation_strength, 0.0)).astype(jnp.float32)


def draw_forcing(key, part):
    shape = (2, EXCITATIONS, AXIAL_POSITIONS, FIELDS, WALL)
    values = jnp.clip(jax.random.normal(key, shape), -6.0, 6.0)
    return values.astype(jnp.float32)


def setup_inputs(seed: int = 0) -> dict:
    seeds = jax.random.split(jax.random.key(seed), 4)
    rate = draw_rate(jax.random.fold_in(seeds[3], 71), 0)
    phase = jnp.clip(jax.random.uniform(seeds[1], (AXIAL_POSITIONS, FIELDS, WALL), jnp.float32, -3.140625, 3.140625), -3.140625, 3.140625)
    forcing = draw_forcing(jax.random.fold_in(seeds[3], 71), 0)
    return {"rate": rate, "phase": phase, "forcing": forcing}


fringe_total = 0.7

def complex_product(left, right):
    return jnp.stack([left[0] * right[0] - left[1] * right[1], left[0] * right[1] + left[1] * right[0]])

def reference(rate, phase, forcing):
    stations = rate.shape[0]
    index = jnp.arange(stations)
    fringe_sponge = jnp.where(index >= stations - STAT_DEV, jnp.float32(fringe_total ** (1.0 / STAT_DEV)), jnp.float32(1.0))
    magnitude = jnp.exp(-rate) * fringe_sponge[:, None, None]
    coeff = jnp.stack([magnitude * jnp.cos(phase), magnitude * jnp.sin(phase)])
    source = jnp.sqrt(-jnp.expm1(-2.0 * rate)) * forcing
    coeff_seq = jnp.moveaxis(coeff, 1, 0)
    source_seq = jnp.moveaxis(source, 2, 0)

    def march(carry, item):
        step_a, step_b = item
        product, value = carry
        return ((complex_product(step_a, product), complex_product(step_a[:, None], value) + step_b), None)
    start_a = jnp.stack([jnp.ones(rate.shape[1:], jnp.float32), jnp.zeros(rate.shape[1:], jnp.float32)])
    start_b = jnp.zeros(forcing.shape[:2] + rate.shape[1:], jnp.float32)
    (periodic_coefficient, loop_b), _ = lax.scan(march, (start_a, start_b), (coeff_seq, source_seq))
    denom_re = 1.0 - periodic_coefficient[0]
    denom_im = -periodic_coefficient[1]
    scale = denom_re * denom_re + denom_im * denom_im
    closing = complex_product(loop_b, jnp.stack([denom_re, -denom_im])[:, None]) / scale

    def sweep(state, item):
        step_a, step_b = item
        fresh = complex_product(step_a[:, None], state) + step_b
        return (fresh, fresh)
    _, values = lax.scan(sweep, closing, (coeff_seq, source_seq))
    return jnp.moveaxis(values, 0, 2)
```

```python
import functools

import jax
import jax.numpy as jnp
from jax import lax
from jax.experimental import pallas as pl
from jax.experimental.pallas import tpu as pltpu
from jax.sharding import PartitionSpec as P

fringe_total = 0.7
FRINGE_STATIONS = 32
AXES = ("loop", "sub")


def map_kernel(coef_ref, scale_ref, f_ref, out_ref):
    stations = scale_ref.shape[0]
    ex = f_ref.shape[1]

    def step(i, carry):
        pr, pi, xr, xi = carry
        cr = coef_ref[0, i]
        ci = coef_ref[1, i]
        sc = scale_ref[i]
        npr = cr * pr - ci * pi
        npi = cr * pi + ci * pr
        nxr, nxi = [], []
        for e in range(ex):
            nxr.append(cr * xr[e] - ci * xi[e] + sc * f_ref[0, e, i])
            nxi.append(cr * xi[e] + ci * xr[e] + sc * f_ref[1, e, i])
        return npr, npi, tuple(nxr), tuple(nxi)

    shape = scale_ref.shape[1:]
    one = jnp.ones(shape, jnp.float32)
    zero = jnp.zeros(shape, jnp.float32)
    init = (one, zero, (zero,) * ex, (zero,) * ex)
    pr, pi, xr, xi = lax.fori_loop(0, stations, step, init, unroll=8)
    for e in range(ex):
        out_ref[0, e] = xr[e]
        out_ref[1, e] = xi[e]
    out_ref[0, ex] = pr
    out_ref[1, ex] = pi


def march_kernel(coef_ref, scale_ref, f_ref, x0_ref, out_ref):
    stations = scale_ref.shape[0]
    ex = f_ref.shape[1]

    def step(i, carry):
        xr, xi = carry
        cr = coef_ref[0, i]
        ci = coef_ref[1, i]
        sc = scale_ref[i]
        nxr, nxi = [], []
        for e in range(ex):
            r = cr * xr[e] - ci * xi[e] + sc * f_ref[0, e, i]
            m = cr * xi[e] + ci * xr[e] + sc * f_ref[1, e, i]
            out_ref[0, e, i] = r
            out_ref[1, e, i] = m
            nxr.append(r)
            nxi.append(m)
        return tuple(nxr), tuple(nxi)

    init = (tuple(x0_ref[0, e] for e in range(ex)), tuple(x0_ref[1, e] for e in range(ex)))
    lax.fori_loop(0, stations, step, init, unroll=8)


def vmem_call(kernel, out_shape, n_in):
    return pl.pallas_call(
        kernel,
        out_shape=out_shape,
        in_specs=[pl.BlockSpec(memory_space=pltpu.VMEM)] * n_in,
        out_specs=pl.BlockSpec(memory_space=pltpu.VMEM),
    )


def compose(earlier, later):
    ex = earlier.shape[1] - 1
    ar, ai = later[0, ex:], later[1, ex:]
    br, bi = earlier[0], earlier[1]
    nr = ar * br - ai * bi
    ni = ar * bi + ai * br
    offset = jnp.stack([nr[:ex], ni[:ex]]) + later[:, :ex]
    gain = jnp.stack([nr[ex:], ni[ex:]])
    return jnp.concatenate([offset, gain], axis=1)


def shift(value, distance, count):
    return lax.ppermute(value, AXES, [(i, (i + distance) % count) for i in range(count)])


def local(rate, phase, forcing):
    stations, fields, wall = rate.shape
    ex = forcing.shape[1]
    count = lax.axis_size(AXES)
    total = stations * count
    me = lax.axis_index(AXES)
    index = me * stations + jnp.arange(stations)
    sponge = jnp.where(
        index >= total - FRINGE_STATIONS,
        jnp.float32(fringe_total ** (1.0 / FRINGE_STATIONS)),
        jnp.float32(1.0),
    )
    magnitude = jnp.exp(-rate) * sponge[:, None, None]
    coef = jnp.stack([magnitude * jnp.cos(phase), magnitude * jnp.sin(phase)])
    scale = jnp.sqrt(-jnp.expm1(-2.0 * rate))

    own = vmem_call(
        map_kernel, jax.ShapeDtypeStruct((2, ex + 1, fields, wall), jnp.float32), 3
    )(coef, scale, forcing)

    loop_map = shift(own, 1, count)
    reach = 1
    while reach < count:
        loop_map = compose(shift(loop_map, reach, count), loop_map)
        reach *= 2

    gr, gi = loop_map[0, ex], loop_map[1, ex]
    denom_re = 1.0 - gr
    denom_im = -gi
    size = denom_re * denom_re + denom_im * denom_im
    br, bi = loop_map[0, :ex], loop_map[1, :ex]
    entering = jnp.stack(
        [(br * denom_re + bi * denom_im) / size, (bi * denom_re - br * denom_im) / size]
    )

    return vmem_call(
        march_kernel, jax.ShapeDtypeStruct(forcing.shape, jnp.float32), 4
    )(coef, scale, forcing, entering)


def solution(mesh):
    count = mesh.shape["loop"] * mesh.shape["sub"]
    assert count & (count - 1) == 0
    placed = (
        P(AXES, None, None),
        P(AXES, None, None),
        P(None, None, AXES, None, None),
    )
    return jax.shard_map(
        local,
        mesh=mesh,
        in_specs=placed,
        out_specs=P(None, None, AXES, None, None),
        check_vma=False,
    )
```

```python
import functools

import jax
import jax.numpy as jnp
from jax import lax
from jax.experimental import pallas as pl
from jax.experimental.pallas import tpu as pltpu
from jax.sharding import PartitionSpec as P

fringe_total = 0.7
FRINGE_STATIONS = 32
AXES = ("loop", "sub")


def map_kernel(coef_ref, scale_ref, f_ref, out_ref):
    stations = scale_ref.shape[0]
    ex = f_ref.shape[1]

    def step(i, carry):
        pr, pi, xr, xi = carry
        cr = coef_ref[0, i]
        ci = coef_ref[1, i]
        sc = scale_ref[i]
        npr = cr * pr - ci * pi
        npi = cr * pi + ci * pr
        nxr, nxi = [], []
        for e in range(ex):
            nxr.append(cr * xr[e] - ci * xi[e] + sc * f_ref[0, e, i])
            nxi.append(cr * xi[e] + ci * xr[e] + sc * f_ref[1, e, i])
        return npr, npi, tuple(nxr), tuple(nxi)

    shape = scale_ref.shape[1:]
    one = jnp.ones(shape, jnp.float32)
    zero = jnp.zeros(shape, jnp.float32)
    init = (one, zero, (zero,) * ex, (zero,) * ex)
    pr, pi, xr, xi = lax.fori_loop(0, stations, step, init, unroll=8)
    for e in range(ex):
        out_ref[0, e] = xr[e]
        out_ref[1, e] = xi[e]
    out_ref[0, ex] = pr
    out_ref[1, ex] = pi


def march_kernel(coef_ref, scale_ref, f_ref, x0_ref, out_ref):
    stations = scale_ref.shape[0]
    ex = f_ref.shape[1]

    def step(i, carry):
        xr, xi = carry
        cr = coef_ref[0, i]
        ci = coef_ref[1, i]
        sc = scale_ref[i]
        nxr, nxi = [], []
        for e in range(ex):
            r = cr * xr[e] - ci * xi[e] + sc * f_ref[0, e, i]
            m = cr * xi[e] + ci * xr[e] + sc * f_ref[1, e, i]
            out_ref[0, e, i] = r
            out_ref[1, e, i] = m
            nxr.append(r)
            nxi.append(m)
        return tuple(nxr), tuple(nxi)

    init = (tuple(x0_ref[0, e] for e in range(ex)), tuple(x0_ref[1, e] for e in range(ex)))
    lax.fori_loop(0, stations, step, init, unroll=8)


def vmem_call(kernel, out_shape, n_in):
    return pl.pallas_call(
        kernel,
        out_shape=out_shape,
        in_specs=[pl.BlockSpec(memory_space=pltpu.VMEM)] * n_in,
        out_specs=pl.BlockSpec(memory_space=pltpu.VMEM),
    )


MESH = pl.DeviceIdType.MESH


def shifts_of(count):
    out, reach = [1], 1
    while reach < count:
        out.append(reach)
        reach *= 2
    return out


def exchange_kernel(count, subs, own_ref, out_ref, recv, cur, send_sem, recv_sem):
    ex = own_ref.shape[1] - 1
    me = lax.axis_index("loop") * subs + lax.axis_index("sub")
    shifts = shifts_of(count)

    def device(offset):
        t = lax.rem(me + offset + count, count)
        return (t // subs, lax.rem(t, subs))

    partners = sorted({s % count for s in shifts} | {(-s) % count for s in shifts})
    barrier = pltpu.get_barrier_semaphore()
    for p in partners:
        pl.semaphore_signal(barrier, inc=1, device_id=device(p), device_id_type=MESH)
    pl.semaphore_wait(barrier, len(partners))

    for k, s in enumerate(shifts):
        if k == 0:
            src = own_ref
        elif k == 1:
            src = recv.at[0]
        else:
            src = cur.at[k]
        copy = pltpu.make_async_remote_copy(
            src_ref=src,
            dst_ref=recv.at[k],
            send_sem=send_sem.at[k],
            recv_sem=recv_sem.at[k],
            device_id=device(s),
            device_id_type=MESH,
        )
        copy.start()
        copy.wait()
        if k == 0:
            continue
        later = recv.at[0] if k == 1 else cur.at[k]
        earlier = recv.at[k]
        ar, ai = later[0, ex], later[1, ex]
        dst = cur.at[k + 1] if k + 1 < len(shifts) else None
        rows = []
        for j in range(ex + 1):
            br, bi = earlier[0, j], earlier[1, j]
            nr = ar * br - ai * bi
            ni = ar * bi + ai * br
            if j < ex:
                nr = nr + later[0, j]
                ni = ni + later[1, j]
            rows.append((nr, ni))
        if dst is not None:
            for j, (nr, ni) in enumerate(rows):
                dst[0, j] = nr
                dst[1, j] = ni
    gr, gi = rows[ex]
    denom_re = 1.0 - gr
    denom_im = -gi
    size = denom_re * denom_re + denom_im * denom_im
    for j in range(ex):
        br, bi = rows[j]
        out_ref[0, j] = (br * denom_re + bi * denom_im) / size
        out_ref[1, j] = (bi * denom_re - br * denom_im) / size


def entering_state(own, count, subs):
    two, slots, fields, wall = own.shape
    rounds = len(shifts_of(count))
    return pl.pallas_call(
        functools.partial(exchange_kernel, count, subs),
        out_shape=jax.ShapeDtypeStruct((two, slots - 1, fields, wall), jnp.float32),
        in_specs=[pl.BlockSpec(memory_space=pltpu.VMEM)],
        out_specs=pl.BlockSpec(memory_space=pltpu.VMEM),
        scratch_shapes=[
            pltpu.VMEM((rounds,) + own.shape, jnp.float32),
            pltpu.VMEM((rounds,) + own.shape, jnp.float32),
            pltpu.SemaphoreType.DMA((rounds,)),
            pltpu.SemaphoreType.DMA((rounds,)),
        ],
        compiler_params=pltpu.CompilerParams(collective_id=0, has_side_effects=True),
    )(own)


def local(rate, phase, forcing):
    stations, fields, wall = rate.shape
    ex = forcing.shape[1]
    count = lax.axis_size(AXES)
    total = stations * count
    me = lax.axis_index(AXES)
    index = me * stations + jnp.arange(stations)
    sponge = jnp.where(
        index >= total - FRINGE_STATIONS,
        jnp.float32(fringe_total ** (1.0 / FRINGE_STATIONS)),
        jnp.float32(1.0),
    )
    magnitude = jnp.exp(-rate) * sponge[:, None, None]
    coef = jnp.stack([magnitude * jnp.cos(phase), magnitude * jnp.sin(phase)])
    scale = jnp.sqrt(-jnp.expm1(-2.0 * rate))

    own = vmem_call(
        map_kernel, jax.ShapeDtypeStruct((2, ex + 1, fields, wall), jnp.float32), 3
    )(coef, scale, forcing)

    entering = entering_state(own, count, lax.axis_size("sub"))

    return vmem_call(
        march_kernel, jax.ShapeDtypeStruct(forcing.shape, jnp.float32), 4
    )(coef, scale, forcing, entering)


def solution(mesh):
    count = mesh.shape["loop"] * mesh.shape["sub"]
    assert count & (count - 1) == 0
    placed = (
        P(AXES, None, None),
        P(AXES, None, None),
        P(None, None, AXES, None, None),
    )
    return jax.shard_map(
        local,
        mesh=mesh,
        in_specs=placed,
        out_specs=P(None, None, AXES, None, None),
        check_vma=False,
    )
```

```python
import functools

import jax
import jax.numpy as jnp
from jax import lax
from jax.experimental import pallas as pl
from jax.experimental.pallas import tpu as pltpu
from jax.sharding import PartitionSpec as P

fringe_total = 0.7
FRINGE_STATIONS = 32
AXES = ("loop", "sub")


def map_kernel(coef_ref, scale_ref, f_ref, out_ref):
    stations = scale_ref.shape[0]
    ex = f_ref.shape[1]

    def step(i, carry):
        pr, pi, xr, xi = carry
        cr = coef_ref[0, i]
        ci = coef_ref[1, i]
        sc = scale_ref[i]
        npr = cr * pr - ci * pi
        npi = cr * pi + ci * pr
        nxr, nxi = [], []
        for e in range(ex):
            nxr.append(cr * xr[e] - ci * xi[e] + sc * f_ref[0, e, i])
            nxi.append(cr * xi[e] + ci * xr[e] + sc * f_ref[1, e, i])
        return npr, npi, tuple(nxr), tuple(nxi)

    shape = scale_ref.shape[1:]
    one = jnp.ones(shape, jnp.float32)
    zero = jnp.zeros(shape, jnp.float32)
    init = (one, zero, (zero,) * ex, (zero,) * ex)
    pr, pi, xr, xi = lax.fori_loop(0, stations, step, init, unroll=8)
    for e in range(ex):
        out_ref[0, e] = xr[e]
        out_ref[1, e] = xi[e]
    out_ref[0, ex] = pr
    out_ref[1, ex] = pi


def march_kernel(coef_ref, scale_ref, f_ref, x0_ref, out_ref):
    stations = scale_ref.shape[0]
    ex = f_ref.shape[1]

    def step(i, carry):
        xr, xi = carry
        cr = coef_ref[0, i]
        ci = coef_ref[1, i]
        sc = scale_ref[i]
        nxr, nxi = [], []
        for e in range(ex):
            r = cr * xr[e] - ci * xi[e] + sc * f_ref[0, e, i]
            m = cr * xi[e] + ci * xr[e] + sc * f_ref[1, e, i]
            out_ref[0, e, i] = r
            out_ref[1, e, i] = m
            nxr.append(r)
            nxi.append(m)
        return tuple(nxr), tuple(nxi)

    init = (tuple(x0_ref[0, e] for e in range(ex)), tuple(x0_ref[1, e] for e in range(ex)))
    lax.fori_loop(0, stations, step, init, unroll=8)


def vmem_call(kernel, out_shape, n_in):
    return pl.pallas_call(
        kernel,
        out_shape=out_shape,
        in_specs=[pl.BlockSpec(memory_space=pltpu.VMEM)] * n_in,
        out_specs=pl.BlockSpec(memory_space=pltpu.VMEM),
    )


MESH = pl.DeviceIdType.MESH


def rounds_of(count):
    out, reach = [], 1
    while reach < count:
        fan = 4 if count % (reach * 4) == 0 else 2
        out.append((reach, fan))
        reach *= fan
    return out


def slots_of(count):
    slots = []
    for k, (stride, fan) in enumerate(rounds_of(count)):
        for j in range(1, fan + (1 if k == 0 else 0)):
            slots.append((k, j * stride))
    return slots


def exchange_kernel(count, subs, own_ref, out_ref, recv, cur, send_sem, recv_sem):
    ex = own_ref.shape[1] - 1
    me = lax.axis_index("loop") * subs + lax.axis_index("sub")
    rounds = rounds_of(count)
    slots = slots_of(count)

    def device(offset):
        t = lax.rem(me + offset + count, count)
        return (t // subs, lax.rem(t, subs))

    partners = sorted({o % count for _, o in slots} | {(-o) % count for _, o in slots})
    barrier = pltpu.get_barrier_semaphore()
    for p in partners:
        pl.semaphore_signal(barrier, inc=1, device_id=device(p), device_id_type=MESH)
    pl.semaphore_wait(barrier, len(partners))

    def load(ref):
        return [(ref[0, j], ref[1, j]) for j in range(ex + 1)]

    def compose(earlier, later):
        ar, ai = later[ex]
        rows = []
        for j in range(ex + 1):
            br, bi = earlier[j]
            nr = ar * br - ai * bi
            ni = ar * bi + ai * br
            if j < ex:
                nr = nr + later[j][0]
                ni = ni + later[j][1]
            rows.append((nr, ni))
        return rows

    held = None
    for k, (stride, fan) in enumerate(rounds):
        mine = [i for i, (r, _) in enumerate(slots) if r == k]
        src = own_ref if k == 0 else cur.at[k]
        copies = []
        for i in mine:
            copy = pltpu.make_async_remote_copy(
                src_ref=src,
                dst_ref=recv.at[i],
                send_sem=send_sem.at[i],
                recv_sem=recv_sem.at[i],
                device_id=device(slots[i][1]),
                device_id_type=MESH,
            )
            copy.start()
            copies.append(copy)
        for n, (i, copy) in enumerate(zip(mine, copies)):
            copy.wait()
            arrived = load(recv.at[i])
            held = arrived if (k == 0 and n == 0) else compose(arrived, held)
        if k + 1 < len(rounds):
            dst = cur.at[k + 1]
            for j, (nr, ni) in enumerate(held):
                dst[0, j] = nr
                dst[1, j] = ni
            held = load(dst)
    gr, gi = held[ex]
    denom_re = 1.0 - gr
    denom_im = -gi
    size = denom_re * denom_re + denom_im * denom_im
    for j in range(ex):
        br, bi = held[j]
        out_ref[0, j] = (br * denom_re + bi * denom_im) / size
        out_ref[1, j] = (bi * denom_re - br * denom_im) / size


def entering_state(own, count, subs):
    two, slots, fields, wall = own.shape
    n_slots = len(slots_of(count))
    n_rounds = len(rounds_of(count))
    return pl.pallas_call(
        functools.partial(exchange_kernel, count, subs),
        out_shape=jax.ShapeDtypeStruct((two, slots - 1, fields, wall), jnp.float32),
        in_specs=[pl.BlockSpec(memory_space=pltpu.VMEM)],
        out_specs=pl.BlockSpec(memory_space=pltpu.VMEM),
        scratch_shapes=[
            pltpu.VMEM((n_slots,) + own.shape, jnp.float32),
            pltpu.VMEM((n_rounds,) + own.shape, jnp.float32),
            pltpu.SemaphoreType.DMA((n_slots,)),
            pltpu.SemaphoreType.DMA((n_slots,)),
        ],
        compiler_params=pltpu.CompilerParams(collective_id=0, has_side_effects=True),
    )(own)


def local(rate, phase, forcing):
    stations, fields, wall = rate.shape
    ex = forcing.shape[1]
    count = lax.axis_size(AXES)
    total = stations * count
    me = lax.axis_index(AXES)
    index = me * stations + jnp.arange(stations)
    sponge = jnp.where(
        index >= total - FRINGE_STATIONS,
        jnp.float32(fringe_total ** (1.0 / FRINGE_STATIONS)),
        jnp.float32(1.0),
    )
    magnitude = jnp.exp(-rate) * sponge[:, None, None]
    coef = jnp.stack([magnitude * jnp.cos(phase), magnitude * jnp.sin(phase)])
    scale = jnp.sqrt(-jnp.expm1(-2.0 * rate))

    own = vmem_call(
        map_kernel, jax.ShapeDtypeStruct((2, ex + 1, fields, wall), jnp.float32), 3
    )(coef, scale, forcing)

    entering = entering_state(own, count, lax.axis_size("sub"))

    return vmem_call(
        march_kernel, jax.ShapeDtypeStruct(forcing.shape, jnp.float32), 4
    )(coef, scale, forcing, entering)


def solution(mesh):
    count = mesh.shape["loop"] * mesh.shape["sub"]
    assert count & (count - 1) == 0
    placed = (
        P(AXES, None, None),
        P(AXES, None, None),
        P(None, None, AXES, None, None),
    )
    return jax.shard_map(
        local,
        mesh=mesh,
        in_specs=placed,
        out_specs=P(None, None, AXES, None, None),
        check_vma=False,
    )
```

```python
import functools

import jax
import jax.numpy as jnp
from jax import lax
from jax.experimental import pallas as pl
from jax.experimental.pallas import tpu as pltpu
from jax.sharding import PartitionSpec as P

fringe_total = 0.7
FRINGE_STATIONS = 32
AXES = ("loop", "sub")
MESH = pl.DeviceIdType.MESH
LANES = 128


def rounds_of(count):
    out, reach = [], 1
    while reach < count:
        fan = 4 if count % (reach * 4) == 0 else 2
        out.append((reach, fan))
        reach *= fan
    return out


def slots_of(count):
    slots = []
    for k, (stride, fan) in enumerate(rounds_of(count)):
        for j in range(1, fan + (1 if k == 0 else 0)):
            slots.append((k, j * stride))
    return slots


def expm1(x):
    u = jnp.exp(x)
    return jnp.where(u == 1.0, x, (u - 1.0) * x / jnp.log(u))


def fetch(srcs, bufs, sems):
    copies = []
    for n, (src, buf) in enumerate(zip(srcs, bufs)):
        for q in range(buf.shape[0]):
            copy = pltpu.make_async_copy(
                src.at[:, pl.ds(q * LANES, LANES)], buf.at[q], sems.at[n * buf.shape[0] + q]
            )
            copy.start()
            copies.append(copy)
    return copies


def station(buf, i, fields, stations):
    rows = pl.ds(i, fields, stride=stations)
    return jnp.concatenate([buf[q, rows, :] for q in range(buf.shape[0])], axis=1)


def map_kernel(count, subs, rate_hbm, phase_hbm, f_hbm, coef_ref, x0_ref,
               rbuf, pbuf, fbuf, in_sem, tmp, pack, recv, cur, send_sem, recv_sem):
    ex = x0_ref.shape[1]
    stations, fields, wall = coef_ref.shape[1:]
    chunks = wall // LANES
    copies = fetch(
        [rate_hbm, phase_hbm] + [f_hbm.at[n] for n in range(2 * ex)],
        [rbuf, pbuf] + [fbuf.at[n] for n in range(2 * ex)],
        in_sem,
    )
    me = lax.axis_index("loop") * subs + lax.axis_index("sub")
    rounds = rounds_of(count)
    slots = slots_of(count)

    def device(offset):
        t = lax.rem(me + offset + count, count)
        return (t // subs, lax.rem(t, subs))

    partners = sorted({o % count for _, o in slots} | {(-o) % count for _, o in slots})
    barrier = pltpu.get_barrier_semaphore()
    for p in partners:
        pl.semaphore_signal(barrier, inc=1, device_id=device(p), device_id_type=MESH)

    first_fringe = count * stations - FRINGE_STATIONS
    damp = jnp.float32(fringe_total ** (1.0 / FRINGE_STATIONS))
    for copy in copies:
        copy.wait()

    def step(i, carry):
        pr, pi, xr, xi = carry
        r = station(rbuf, i, fields, stations)
        ph = station(pbuf, i, fields, stations)
        sponge = jnp.where(me * stations + i >= first_fringe, damp, jnp.float32(1.0))
        mag = jnp.exp(-r) * sponge
        cr = mag * jnp.cos(ph)
        ci = mag * jnp.sin(ph)
        sc = jnp.sqrt(-expm1(-2.0 * r))
        coef_ref[0, i] = cr
        coef_ref[1, i] = ci
        coef_ref[2, i] = sc
        npr = cr * pr - ci * pi
        npi = cr * pi + ci * pr
        nxr, nxi = [], []
        for e in range(ex):
            fr = station(fbuf.at[e], i, fields, stations)
            fi = station(fbuf.at[ex + e], i, fields, stations)
            nxr.append(cr * xr[e] - ci * xi[e] + sc * fr)
            nxi.append(cr * xi[e] + ci * xr[e] + sc * fi)
        return npr, npi, tuple(nxr), tuple(nxi)

    shape = (fields, wall)
    one = jnp.ones(shape, jnp.float32)
    zero = jnp.zeros(shape, jnp.float32)
    init = (one, zero, (zero,) * ex, (zero,) * ex)
    pr, pi, xr, xi = lax.fori_loop(0, stations, step, init, unroll=4)

    values = [(xr[e], xi[e]) for e in range(ex)] + [(pr, pi)]
    for j, pair in enumerate(values):
        for c in range(2):
            tmp[...] = pair[c]
            for f in range(fields):
                for q in range(chunks):
                    pack[c, j, pl.ds(f * chunks + q, 1), :] = tmp[
                        pl.ds(f, 1), pl.ds(q * LANES, LANES)
                    ]

    pl.semaphore_wait(barrier, len(partners))

    def load(ref):
        return [(ref[0, j], ref[1, j]) for j in range(ex + 1)]

    def compose(earlier, later):
        ar, ai = later[ex]
        out = []
        for j in range(ex + 1):
            br, bi = earlier[j]
            nr = ar * br - ai * bi
            ni = ar * bi + ai * br
            if j < ex:
                nr = nr + later[j][0]
                ni = ni + later[j][1]
            out.append((nr, ni))
        return out

    held = None
    for k in range(len(rounds)):
        mine = [i for i, (r, _) in enumerate(slots) if r == k]
        src = pack if k == 0 else cur.at[k]
        copies = []
        for i in mine:
            copy = pltpu.make_async_remote_copy(
                src_ref=src,
                dst_ref=recv.at[i],
                send_sem=send_sem.at[i],
                recv_sem=recv_sem.at[i],
                device_id=device(slots[i][1]),
                device_id_type=MESH,
            )
            copy.start()
            copies.append(copy)
        for n, (i, copy) in enumerate(zip(mine, copies)):
            copy.wait()
            arrived = load(recv.at[i])
            held = arrived if (k == 0 and n == 0) else compose(arrived, held)
        if k + 1 < len(rounds):
            dst = cur.at[k + 1]
            for j, (nr, ni) in enumerate(held):
                dst[0, j] = nr
                dst[1, j] = ni
            held = load(dst)

    gr, gi = held[ex]
    denom_re = 1.0 - gr
    denom_im = -gi
    size = denom_re * denom_re + denom_im * denom_im
    ent = cur.at[0]
    for j in range(ex):
        br, bi = held[j]
        ent[0, j] = (br * denom_re + bi * denom_im) / size
        ent[1, j] = (bi * denom_re - br * denom_im) / size
    for c in range(2):
        for e in range(ex):
            for f in range(fields):
                for q in range(chunks):
                    x0_ref[c, e, pl.ds(f, 1), pl.ds(q * LANES, LANES)] = ent[
                        c, e, pl.ds(f * chunks + q, 1), :
                    ]


def march_kernel(coef_ref, f_hbm, x0_ref, out_hbm, fbuf, obuf, in_sem, out_sem):
    ex = x0_ref.shape[1]
    stations, fields = coef_ref.shape[1:3]
    chunks = fbuf.shape[1]
    copies = fetch([f_hbm.at[n] for n in range(2 * ex)], [fbuf.at[n] for n in range(2 * ex)], in_sem)
    for copy in copies:
        copy.wait()

    def put(n, i, value):
        rows = pl.ds(i, fields, stride=stations)
        for q in range(chunks):
            obuf[n, q, rows, :] = value[:, q * LANES:(q + 1) * LANES]

    def step(i, carry):
        xr, xi = carry
        cr = coef_ref[0, i]
        ci = coef_ref[1, i]
        sc = coef_ref[2, i]
        nxr, nxi = [], []
        for e in range(ex):
            fr = station(fbuf.at[e], i, fields, stations)
            fi = station(fbuf.at[ex + e], i, fields, stations)
            r = cr * xr[e] - ci * xi[e] + sc * fr
            m = cr * xi[e] + ci * xr[e] + sc * fi
            put(e, i, r)
            put(ex + e, i, m)
            nxr.append(r)
            nxi.append(m)
        return tuple(nxr), tuple(nxi)

    init = (tuple(x0_ref[0, e] for e in range(ex)), tuple(x0_ref[1, e] for e in range(ex)))
    lax.fori_loop(0, stations, step, init, unroll=4)
    copies = []
    for n in range(2 * ex):
        for q in range(chunks):
            copy = pltpu.make_async_copy(
                obuf.at[n, q], out_hbm.at[n, :, pl.ds(q * LANES, LANES)], out_sem.at[n * chunks + q]
            )
            copy.start()
            copies.append(copy)
    for copy in copies:
        copy.wait()


def local(rate, phase, forcing):
    stations, fields, wall = rate.shape
    two, ex = forcing.shape[:2]
    count = lax.axis_size(AXES)
    subs = lax.axis_size("sub")
    rate_t = jnp.transpose(rate, (1, 0, 2)).reshape(fields * stations, wall)
    phase_t = jnp.transpose(phase, (1, 0, 2)).reshape(fields * stations, wall)
    forcing_t = jnp.transpose(forcing, (0, 1, 3, 2, 4)).reshape(
        two * ex, fields * stations, wall
    )
    n_slots = len(slots_of(count))
    n_rounds = len(rounds_of(count))
    packed = (2, ex + 1, fields * wall // LANES, LANES)
    vmem = pl.BlockSpec(memory_space=pltpu.VMEM)
    hbm = pl.BlockSpec(memory_space=pl.ANY)
    chunks = wall // LANES
    slab = (fields * stations, LANES)
    fbuf = pltpu.VMEM((two * ex, chunks) + slab, jnp.float32)
    coef, x0 = pl.pallas_call(
        functools.partial(map_kernel, count, subs),
        out_shape=(
            jax.ShapeDtypeStruct((3, stations, fields, wall), jnp.float32),
            jax.ShapeDtypeStruct((2, ex, fields, wall), jnp.float32),
        ),
        in_specs=[hbm] * 3,
        out_specs=(vmem, vmem),
        scratch_shapes=[
            pltpu.VMEM((chunks,) + slab, jnp.float32),
            pltpu.VMEM((chunks,) + slab, jnp.float32),
            fbuf,
            pltpu.SemaphoreType.DMA(((2 + two * ex) * chunks,)),
            pltpu.VMEM((fields, wall), jnp.float32),
            pltpu.VMEM(packed, jnp.float32),
            pltpu.VMEM((n_slots,) + packed, jnp.float32),
            pltpu.VMEM((n_rounds,) + packed, jnp.float32),
            pltpu.SemaphoreType.DMA((n_slots,)),
            pltpu.SemaphoreType.DMA((n_slots,)),
        ],
        compiler_params=pltpu.CompilerParams(collective_id=0, has_side_effects=True),
    )(rate_t, phase_t, forcing_t)
    out_t = pl.pallas_call(
        march_kernel,
        out_shape=jax.ShapeDtypeStruct(forcing_t.shape, jnp.float32),
        in_specs=[vmem, hbm, vmem],
        out_specs=hbm,
        scratch_shapes=[
            fbuf,
            fbuf,
            pltpu.SemaphoreType.DMA((two * ex * chunks,)),
            pltpu.SemaphoreType.DMA((two * ex * chunks,)),
        ],
    )(coef, forcing_t, x0)
    return jnp.transpose(out_t.reshape(two, ex, fields, stations, wall), (0, 1, 3, 2, 4))


def solution(mesh):
    count = mesh.shape["loop"] * mesh.shape["sub"]
    assert count & (count - 1) == 0
    placed = (
        P(AXES, None, None),
        P(AXES, None, None),
        P(None, None, AXES, None, None),
    )
    return jax.shard_map(
        local,
        mesh=mesh,
        in_specs=placed,
        out_specs=P(None, None, AXES, None, None),
        check_vma=False,
    )
```

```python
import functools

import jax
import jax.numpy as jnp
from jax import lax
from jax.experimental import pallas as pl
from jax.experimental.pallas import tpu as pltpu
from jax.sharding import PartitionSpec as P

fringe_total = 0.7
FRINGE_STATIONS = 32
AXES = ("loop", "sub")
MESH = pl.DeviceIdType.MESH
LANES = 128


def rounds_of(count):
    out, reach = [], 1
    while reach < count:
        fan = 4 if count % (reach * 4) == 0 else 2
        out.append((reach, fan))
        reach *= fan
    return out


def slots_of(count):
    slots = []
    for k, (stride, fan) in enumerate(rounds_of(count)):
        for j in range(1, fan + (1 if k == 0 else 0)):
            slots.append((k, j * stride))
    return slots


def expm1(x):
    u = jnp.exp(x)
    return jnp.where(u == 1.0, x, (u - 1.0) * x / jnp.log(u))


def fetch(srcs, bufs, sems):
    copies = []
    for n, (src, buf) in enumerate(zip(srcs, bufs)):
        for q in range(buf.shape[0]):
            copy = pltpu.make_async_copy(
                src.at[:, pl.ds(q * LANES, LANES)], buf.at[q], sems.at[n * buf.shape[0] + q]
            )
            copy.start()
            copies.append(copy)
    return copies


def station(buf, i, fields, stations):
    rows = pl.ds(i, fields, stride=stations)
    return jnp.concatenate([buf[q, rows, :] for q in range(buf.shape[0])], axis=1)


def resolvent_kernel(count, subs, rate_hbm, phase_hbm, f_hbm, out_hbm,
                     rbuf, pbuf, fbuf, in_sem, coef_ref, x0_ref, qbuf, gbuf, out_sem,
                     tmp, pack, recv, cur, send_sem, recv_sem):
    ex = x0_ref.shape[1]
    stations, fields, wall = coef_ref.shape[1:]
    chunks = wall // LANES
    copies = fetch(
        [rate_hbm, phase_hbm] + [f_hbm.at[n] for n in range(2 * ex)],
        [rbuf, pbuf] + [fbuf.at[n] for n in range(2 * ex)],
        in_sem,
    )
    me = lax.axis_index("loop") * subs + lax.axis_index("sub")
    rounds = rounds_of(count)
    slots = slots_of(count)

    def device(offset):
        t = lax.rem(me + offset + count, count)
        return (t // subs, lax.rem(t, subs))

    partners = sorted({o % count for _, o in slots} | {(-o) % count for _, o in slots})
    barrier = pltpu.get_barrier_semaphore()
    for p in partners:
        pl.semaphore_signal(barrier, inc=1, device_id=device(p), device_id_type=MESH)

    first_fringe = count * stations - FRINGE_STATIONS
    damp = jnp.float32(fringe_total ** (1.0 / FRINGE_STATIONS))
    for copy in copies:
        copy.wait()

    def step(i, carry):
        pr, pi, xr, xi = carry
        r = station(rbuf, i, fields, stations)
        ph = station(pbuf, i, fields, stations)
        sponge = jnp.where(me * stations + i >= first_fringe, damp, jnp.float32(1.0))
        mag = jnp.exp(-r) * sponge
        cr = mag * jnp.cos(ph)
        ci = mag * jnp.sin(ph)
        sc = jnp.sqrt(-expm1(-2.0 * r))
        coef_ref[0, i] = cr
        coef_ref[1, i] = ci
        coef_ref[2, i] = sc
        npr = cr * pr - ci * pi
        npi = cr * pi + ci * pr
        nxr, nxi = [], []
        for e in range(ex):
            fr = station(fbuf.at[e], i, fields, stations)
            fi = station(fbuf.at[ex + e], i, fields, stations)
            nxr.append(cr * xr[e] - ci * xi[e] + sc * fr)
            nxi.append(cr * xi[e] + ci * xr[e] + sc * fi)
        return npr, npi, tuple(nxr), tuple(nxi)

    shape = (fields, wall)
    one = jnp.ones(shape, jnp.float32)
    zero = jnp.zeros(shape, jnp.float32)
    init = (one, zero, (zero,) * ex, (zero,) * ex)
    pr, pi, xr, xi = lax.fori_loop(0, stations, step, init, unroll=4)

    values = [(xr[e], xi[e]) for e in range(ex)] + [(pr, pi)]
    for j, pair in enumerate(values):
        for c in range(2):
            tmp[...] = pair[c]
            for f in range(fields):
                for q in range(chunks):
                    pack[c, j, pl.ds(f * chunks + q, 1), :] = tmp[
                        pl.ds(f, 1), pl.ds(q * LANES, LANES)
                    ]

    pl.semaphore_wait(barrier, len(partners))

    def put(buf, n, i, value):
        rows = pl.ds(i, fields, stride=stations)
        for q in range(chunks):
            buf[n, q, rows, :] = value[:, q * LANES:(q + 1) * LANES]

    def local_march():
        def step(i, carry):
            pr, pi, xr, xi = carry
            cr = coef_ref[0, i]
            ci = coef_ref[1, i]
            sc = coef_ref[2, i]
            npr = cr * pr - ci * pi
            npi = cr * pi + ci * pr
            put(gbuf, 0, i, npr)
            put(gbuf, 1, i, npi)
            nxr, nxi = [], []
            for e in range(ex):
                fr = station(fbuf.at[e], i, fields, stations)
                fi = station(fbuf.at[ex + e], i, fields, stations)
                r = cr * xr[e] - ci * xi[e] + sc * fr
                m = cr * xi[e] + ci * xr[e] + sc * fi
                put(qbuf, e, i, r)
                put(qbuf, ex + e, i, m)
                nxr.append(r)
                nxi.append(m)
            return npr, npi, tuple(nxr), tuple(nxi)

        lax.fori_loop(0, stations, step, init, unroll=4)

    def load(ref):
        return [(ref[0, j], ref[1, j]) for j in range(ex + 1)]

    def compose(earlier, later):
        ar, ai = later[ex]
        out = []
        for j in range(ex + 1):
            br, bi = earlier[j]
            nr = ar * br - ai * bi
            ni = ar * bi + ai * br
            if j < ex:
                nr = nr + later[j][0]
                ni = ni + later[j][1]
            out.append((nr, ni))
        return out

    held = None
    for k in range(len(rounds)):
        mine = [i for i, (r, _) in enumerate(slots) if r == k]
        src = pack if k == 0 else cur.at[k]
        copies = []
        for i in mine:
            copy = pltpu.make_async_remote_copy(
                src_ref=src,
                dst_ref=recv.at[i],
                send_sem=send_sem.at[i],
                recv_sem=recv_sem.at[i],
                device_id=device(slots[i][1]),
                device_id_type=MESH,
            )
            copy.start()
            copies.append(copy)
        if k == 0:
            local_march()
        for n, (i, copy) in enumerate(zip(mine, copies)):
            copy.wait()
            arrived = load(recv.at[i])
            held = arrived if (k == 0 and n == 0) else compose(arrived, held)
        if k + 1 < len(rounds):
            dst = cur.at[k + 1]
            for j, (nr, ni) in enumerate(held):
                dst[0, j] = nr
                dst[1, j] = ni
            held = load(dst)

    gr, gi = held[ex]
    denom_re = 1.0 - gr
    denom_im = -gi
    size = denom_re * denom_re + denom_im * denom_im
    ent = cur.at[0]
    for j in range(ex):
        br, bi = held[j]
        ent[0, j] = (br * denom_re + bi * denom_im) / size
        ent[1, j] = (bi * denom_re - br * denom_im) / size
    for c in range(2):
        for e in range(ex):
            for f in range(fields):
                for q in range(chunks):
                    x0_ref[c, e, pl.ds(f, 1), pl.ds(q * LANES, LANES)] = ent[
                        c, e, pl.ds(f * chunks + q, 1), :
                    ]

    copies = []
    for e in range(ex):
        for q in range(chunks):
            lanes = pl.ds(q * LANES, LANES)
            for f in range(fields):
                rows = pl.ds(f * stations, stations)
                xr = x0_ref[0, e, pl.ds(f, 1), lanes]
                xi = x0_ref[1, e, pl.ds(f, 1), lanes]
                gr = gbuf[0, q, rows, :]
                gi = gbuf[1, q, rows, :]
                qbuf[e, q, rows, :] = qbuf[e, q, rows, :] + (gr * xr - gi * xi)
                qbuf[ex + e, q, rows, :] = qbuf[ex + e, q, rows, :] + (gr * xi + gi * xr)
            for n in (e, ex + e):
                copy = pltpu.make_async_copy(
                    qbuf.at[n, q], out_hbm.at[n, :, lanes], out_sem.at[n * chunks + q]
                )
                copy.start()
                copies.append(copy)
    for copy in copies:
        copy.wait()


def local(rate, phase, forcing):
    stations, fields, wall = rate.shape
    two, ex = forcing.shape[:2]
    count = lax.axis_size(AXES)
    subs = lax.axis_size("sub")
    rate_t = jnp.transpose(rate, (1, 0, 2)).reshape(fields * stations, wall)
    phase_t = jnp.transpose(phase, (1, 0, 2)).reshape(fields * stations, wall)
    forcing_t = jnp.transpose(forcing, (0, 1, 3, 2, 4)).reshape(
        two * ex, fields * stations, wall
    )
    n_slots = len(slots_of(count))
    n_rounds = len(rounds_of(count))
    packed = (2, ex + 1, fields * wall // LANES, LANES)
    vmem = pl.BlockSpec(memory_space=pltpu.VMEM)
    hbm = pl.BlockSpec(memory_space=pl.ANY)
    chunks = wall // LANES
    slab = (fields * stations, LANES)
    fbuf = pltpu.VMEM((two * ex, chunks) + slab, jnp.float32)
    out_t = pl.pallas_call(
        functools.partial(resolvent_kernel, count, subs),
        out_shape=jax.ShapeDtypeStruct(forcing_t.shape, jnp.float32),
        in_specs=[hbm] * 3,
        out_specs=hbm,
        scratch_shapes=[
            pltpu.VMEM((chunks,) + slab, jnp.float32),
            pltpu.VMEM((chunks,) + slab, jnp.float32),
            fbuf,
            pltpu.SemaphoreType.DMA(((2 + two * ex) * chunks,)),
            pltpu.VMEM((3, stations, fields, wall), jnp.float32),
            pltpu.VMEM((2, ex, fields, wall), jnp.float32),
            fbuf,
            pltpu.VMEM((2, chunks) + slab, jnp.float32),
            pltpu.SemaphoreType.DMA((two * ex * chunks,)),
            pltpu.VMEM((fields, wall), jnp.float32),
            pltpu.VMEM(packed, jnp.float32),
            pltpu.VMEM((n_slots,) + packed, jnp.float32),
            pltpu.VMEM((n_rounds,) + packed, jnp.float32),
            pltpu.SemaphoreType.DMA((n_slots,)),
            pltpu.SemaphoreType.DMA((n_slots,)),
        ],
        compiler_params=pltpu.CompilerParams(collective_id=0, has_side_effects=True),
    )(rate_t, phase_t, forcing_t)
    return jnp.transpose(out_t.reshape(two, ex, fields, stations, wall), (0, 1, 3, 2, 4))


def solution(mesh):
    count = mesh.shape["loop"] * mesh.shape["sub"]
    assert count & (count - 1) == 0
    placed = (
        P(AXES, None, None),
        P(AXES, None, None),
        P(None, None, AXES, None, None),
    )
    return jax.shard_map(
        local,
        mesh=mesh,
        in_specs=placed,
        out_specs=P(None, None, AXES, None, None),
        check_vma=False,
    )
```

```python
import functools

import jax
import jax.numpy as jnp
from jax import lax
from jax.experimental import pallas as pl
from jax.experimental.pallas import tpu as pltpu
from jax.sharding import PartitionSpec as P

fringe_total = 0.7
FRINGE_STATIONS = 32
AXES = ("loop", "sub")
MESH = pl.DeviceIdType.MESH
LANES = 128


def rounds_of(count):
    out, reach = [], 1
    while reach < count:
        fan = 4 if count % (reach * 4) == 0 else 2
        out.append((reach, fan))
        reach *= fan
    return out


def slots_of(count):
    slots = []
    for k, (stride, fan) in enumerate(rounds_of(count)):
        for j in range(1, fan + (1 if k == 0 else 0)):
            slots.append((k, j * stride))
    return slots


def expm1(x):
    u = jnp.exp(x)
    return jnp.where(u == 1.0, x, (u - 1.0) * x / jnp.log(u))


def fetch(srcs, bufs, sems):
    copies = []
    for n, (src, buf) in enumerate(zip(srcs, bufs)):
        for q in range(buf.shape[0]):
            copy = pltpu.make_async_copy(
                src.at[:, pl.ds(q * LANES, LANES)], buf.at[q], sems.at[n * buf.shape[0] + q]
            )
            copy.start()
            copies.append(copy)
    return copies


def station(buf, i, fields, stations):
    rows = pl.ds(i, fields, stride=stations)
    return jnp.concatenate([buf[q, rows, :] for q in range(buf.shape[0])], axis=1)


def resolvent_kernel(count, subs, rate_hbm, phase_hbm, f_hbm, out_hbm, x0_ref,
                     rbuf, pbuf, fbuf, in_sem, coef_ref, qbuf, gbuf, out_sem,
                     tmp, pack, recv, cur, send_sem, recv_sem):
    ex = x0_ref.shape[1]
    stations, fields, wall = coef_ref.shape[1:]
    chunks = wall // LANES
    copies = fetch(
        [rate_hbm, phase_hbm] + [f_hbm.at[n] for n in range(2 * ex)],
        [rbuf, pbuf] + [fbuf.at[n] for n in range(2 * ex)],
        in_sem,
    )
    me = lax.axis_index("loop") * subs + lax.axis_index("sub")
    rounds = rounds_of(count)
    slots = slots_of(count)

    def device(offset):
        t = lax.rem(me + offset + count, count)
        return (t // subs, lax.rem(t, subs))

    partners = sorted({o % count for _, o in slots} | {(-o) % count for _, o in slots})
    barrier = pltpu.get_barrier_semaphore()
    for p in partners:
        pl.semaphore_signal(barrier, inc=1, device_id=device(p), device_id_type=MESH)

    first_fringe = count * stations - FRINGE_STATIONS
    damp = jnp.float32(fringe_total ** (1.0 / FRINGE_STATIONS))
    for copy in copies:
        copy.wait()

    def step(i, carry):
        pr, pi, xr, xi = carry
        r = station(rbuf, i, fields, stations)
        ph = station(pbuf, i, fields, stations)
        sponge = jnp.where(me * stations + i >= first_fringe, damp, jnp.float32(1.0))
        mag = jnp.exp(-r) * sponge
        cr = mag * jnp.cos(ph)
        ci = mag * jnp.sin(ph)
        sc = jnp.sqrt(-expm1(-2.0 * r))
        coef_ref[0, i] = cr
        coef_ref[1, i] = ci
        coef_ref[2, i] = sc
        npr = cr * pr - ci * pi
        npi = cr * pi + ci * pr
        nxr, nxi = [], []
        for e in range(ex):
            fr = station(fbuf.at[e], i, fields, stations)
            fi = station(fbuf.at[ex + e], i, fields, stations)
            nxr.append(cr * xr[e] - ci * xi[e] + sc * fr)
            nxi.append(cr * xi[e] + ci * xr[e] + sc * fi)
        return npr, npi, tuple(nxr), tuple(nxi)

    shape = (fields, wall)
    one = jnp.ones(shape, jnp.float32)
    zero = jnp.zeros(shape, jnp.float32)
    init = (one, zero, (zero,) * ex, (zero,) * ex)
    pr, pi, xr, xi = lax.fori_loop(0, stations, step, init, unroll=4)

    values = [(xr[e], xi[e]) for e in range(ex)] + [(pr, pi)]
    for j, pair in enumerate(values):
        for c in range(2):
            tmp[...] = pair[c]
            for f in range(fields):
                for q in range(chunks):
                    pack[c, j, pl.ds(f * chunks + q, 1), :] = tmp[
                        pl.ds(f, 1), pl.ds(q * LANES, LANES)
                    ]

    pl.semaphore_wait(barrier, len(partners))

    def put(buf, n, i, value):
        rows = pl.ds(i, fields, stride=stations)
        for q in range(chunks):
            buf[n, q, rows, :] = value[:, q * LANES:(q + 1) * LANES]

    def local_march():
        def step(i, carry):
            pr, pi, xr, xi = carry
            cr = coef_ref[0, i]
            ci = coef_ref[1, i]
            sc = coef_ref[2, i]
            npr = cr * pr - ci * pi
            npi = cr * pi + ci * pr
            put(gbuf, 0, i, npr)
            put(gbuf, 1, i, npi)
            nxr, nxi = [], []
            for e in range(ex):
                fr = station(fbuf.at[e], i, fields, stations)
                fi = station(fbuf.at[ex + e], i, fields, stations)
                r = cr * xr[e] - ci * xi[e] + sc * fr
                m = cr * xi[e] + ci * xr[e] + sc * fi
                put(qbuf, e, i, r)
                put(qbuf, ex + e, i, m)
                nxr.append(r)
                nxi.append(m)
            return npr, npi, tuple(nxr), tuple(nxi)

        lax.fori_loop(0, stations, step, init, unroll=4)
        sends = []
        for n in range(2 * ex + 2):
            for q in range(chunks):
                src = qbuf.at[n, q] if n < 2 * ex else gbuf.at[n - 2 * ex, q]
                copy = pltpu.make_async_copy(
                    src, out_hbm.at[n, :, pl.ds(q * LANES, LANES)], out_sem.at[n * chunks + q]
                )
                copy.start()
                sends.append(copy)
        return sends

    def load(ref):
        return [(ref[0, j], ref[1, j]) for j in range(ex + 1)]

    def compose(earlier, later):
        ar, ai = later[ex]
        out = []
        for j in range(ex + 1):
            br, bi = earlier[j]
            nr = ar * br - ai * bi
            ni = ar * bi + ai * br
            if j < ex:
                nr = nr + later[j][0]
                ni = ni + later[j][1]
            out.append((nr, ni))
        return out

    held = None
    for k in range(len(rounds)):
        mine = [i for i, (r, _) in enumerate(slots) if r == k]
        src = pack if k == 0 else cur.at[k]
        copies = []
        for i in mine:
            copy = pltpu.make_async_remote_copy(
                src_ref=src,
                dst_ref=recv.at[i],
                send_sem=send_sem.at[i],
                recv_sem=recv_sem.at[i],
                device_id=device(slots[i][1]),
                device_id_type=MESH,
            )
            copy.start()
            copies.append(copy)
        if k == 0:
            stored = local_march()
        for n, (i, copy) in enumerate(zip(mine, copies)):
            copy.wait()
            arrived = load(recv.at[i])
            held = arrived if (k == 0 and n == 0) else compose(arrived, held)
        if k + 1 < len(rounds):
            dst = cur.at[k + 1]
            for j, (nr, ni) in enumerate(held):
                dst[0, j] = nr
                dst[1, j] = ni
            held = load(dst)

    gr, gi = held[ex]
    denom_re = 1.0 - gr
    denom_im = -gi
    size = denom_re * denom_re + denom_im * denom_im
    ent = cur.at[0]
    for j in range(ex):
        br, bi = held[j]
        ent[0, j] = (br * denom_re + bi * denom_im) / size
        ent[1, j] = (bi * denom_re - br * denom_im) / size
    for c in range(2):
        for e in range(ex):
            for f in range(fields):
                for q in range(chunks):
                    x0_ref[c, e, pl.ds(f, 1), pl.ds(q * LANES, LANES)] = ent[
                        c, e, pl.ds(f * chunks + q, 1), :
                    ]

    for copy in stored:
        copy.wait()


def response_kernel(qg_hbm, x0_ref, out_hbm, qg, obuf, in_sem, out_sem):
    ex = x0_ref.shape[1]
    fields = x0_ref.shape[2]
    stations = qg.shape[1] // fields
    blocks = qg.shape[0]
    fetches = []
    for n in range(blocks):
        copy = pltpu.make_async_copy(qg_hbm.at[n], qg.at[n], in_sem.at[n])
        copy.start()
        fetches.append(copy)
    fetches[2 * ex].wait()
    fetches[2 * ex + 1].wait()
    sends = []
    for e in range(ex):
        fetches[e].wait()
        fetches[ex + e].wait()
        for f in range(fields):
            rows = pl.ds(f * stations, stations)
            xr = x0_ref[0, e, pl.ds(f, 1), :]
            xi = x0_ref[1, e, pl.ds(f, 1), :]
            gr = qg[2 * ex, rows, :]
            gi = qg[2 * ex + 1, rows, :]
            obuf[e, rows, :] = qg[e, rows, :] + (gr * xr - gi * xi)
            obuf[ex + e, rows, :] = qg[ex + e, rows, :] + (gr * xi + gi * xr)
        for n in (e, ex + e):
            copy = pltpu.make_async_copy(obuf.at[n], out_hbm.at[n], out_sem.at[n])
            copy.start()
            sends.append(copy)
    for copy in sends:
        copy.wait()


def local(rate, phase, forcing):
    stations, fields, wall = rate.shape
    two, ex = forcing.shape[:2]
    count = lax.axis_size(AXES)
    subs = lax.axis_size("sub")
    rate_t = jnp.transpose(rate, (1, 0, 2)).reshape(fields * stations, wall)
    phase_t = jnp.transpose(phase, (1, 0, 2)).reshape(fields * stations, wall)
    forcing_t = jnp.transpose(forcing, (0, 1, 3, 2, 4)).reshape(
        two * ex, fields * stations, wall
    )
    n_slots = len(slots_of(count))
    n_rounds = len(rounds_of(count))
    packed = (2, ex + 1, fields * wall // LANES, LANES)
    vmem = pl.BlockSpec(memory_space=pltpu.VMEM)
    hbm = pl.BlockSpec(memory_space=pl.ANY)
    chunks = wall // LANES
    slab = (fields * stations, LANES)
    fbuf = pltpu.VMEM((two * ex, chunks) + slab, jnp.float32)
    blocks = two * ex + 2
    qg, x0 = pl.pallas_call(
        functools.partial(resolvent_kernel, count, subs),
        out_shape=(
            jax.ShapeDtypeStruct((blocks,) + forcing_t.shape[1:], jnp.float32),
            jax.ShapeDtypeStruct((2, ex, fields, wall), jnp.float32),
        ),
        in_specs=[hbm] * 3,
        out_specs=(hbm, vmem),
        scratch_shapes=[
            pltpu.VMEM((chunks,) + slab, jnp.float32),
            pltpu.VMEM((chunks,) + slab, jnp.float32),
            fbuf,
            pltpu.SemaphoreType.DMA(((2 + two * ex) * chunks,)),
            pltpu.VMEM((3, stations, fields, wall), jnp.float32),
            fbuf,
            pltpu.VMEM((2, chunks) + slab, jnp.float32),
            pltpu.SemaphoreType.DMA((blocks * chunks,)),
            pltpu.VMEM((fields, wall), jnp.float32),
            pltpu.VMEM(packed, jnp.float32),
            pltpu.VMEM((n_slots,) + packed, jnp.float32),
            pltpu.VMEM((n_rounds,) + packed, jnp.float32),
            pltpu.SemaphoreType.DMA((n_slots,)),
            pltpu.SemaphoreType.DMA((n_slots,)),
        ],
        compiler_params=pltpu.CompilerParams(collective_id=0, has_side_effects=True),
    )(rate_t, phase_t, forcing_t)
    out_t = pl.pallas_call(
        response_kernel,
        out_shape=jax.ShapeDtypeStruct(forcing_t.shape, jnp.float32),
        in_specs=[hbm, vmem],
        out_specs=hbm,
        scratch_shapes=[
            pltpu.VMEM(qg.shape, jnp.float32),
            pltpu.VMEM(forcing_t.shape, jnp.float32),
            pltpu.SemaphoreType.DMA((blocks,)),
            pltpu.SemaphoreType.DMA((two * ex,)),
        ],
    )(qg, x0)
    return jnp.transpose(out_t.reshape(two, ex, fields, stations, wall), (0, 1, 3, 2, 4))


def solution(mesh):
    count = mesh.shape["loop"] * mesh.shape["sub"]
    assert count & (count - 1) == 0
    placed = (
        P(AXES, None, None),
        P(AXES, None, None),
        P(None, None, AXES, None, None),
    )
    return jax.shard_map(
        local,
        mesh=mesh,
        in_specs=placed,
        out_specs=P(None, None, AXES, None, None),
        check_vma=False,
    )
```

```python
import functools

import jax
import jax.numpy as jnp
from jax import lax
from jax.experimental import pallas as pl
from jax.experimental.pallas import tpu as pltpu
from jax.sharding import PartitionSpec as P

fringe_total = 0.7
FRINGE_STATIONS = 32
AXES = ("loop", "sub")
MESH = pl.DeviceIdType.MESH
LANES = 128


def rounds_of(count):
    out, reach = [], 1
    while reach < count:
        fan = 4 if count % (reach * 4) == 0 else 2
        out.append((reach, fan))
        reach *= fan
    return out


def slots_of(count):
    slots = []
    for k, (stride, fan) in enumerate(rounds_of(count)):
        for j in range(1, fan + (1 if k == 0 else 0)):
            slots.append((k, j * stride))
    return slots


def expm1(x):
    u = jnp.exp(x)
    return jnp.where(u == 1.0, x, (u - 1.0) * x / jnp.log(u))


def fetch(srcs, bufs, sems):
    copies = []
    for n, (src, buf) in enumerate(zip(srcs, bufs)):
        for q in range(buf.shape[0]):
            copy = pltpu.make_async_copy(
                src.at[:, pl.ds(q * LANES, LANES)], buf.at[q], sems.at[n * buf.shape[0] + q]
            )
            copy.start()
            copies.append(copy)
    return copies


def station(buf, i, fields, stations):
    rows = pl.ds(i, fields, stride=stations)
    return jnp.concatenate([buf[q, rows, :] for q in range(buf.shape[0])], axis=1)


def resolvent_kernel(count, subs, rate_hbm, phase_hbm, f_hbm, out_hbm, gr_hbm, gi_hbm, x0_ref,
                     rbuf, pbuf, fbuf, in_sem, coef_ref, qbuf, gbuf, out_sem,
                     tmp, pack, recv, cur, send_sem, recv_sem):
    ex = x0_ref.shape[1]
    stations, fields, wall = coef_ref.shape[1:]
    chunks = wall // LANES
    copies = fetch(
        [rate_hbm, phase_hbm] + [f_hbm.at[n] for n in range(2 * ex)],
        [rbuf, pbuf] + [fbuf.at[n] for n in range(2 * ex)],
        in_sem,
    )
    me = lax.axis_index("loop") * subs + lax.axis_index("sub")
    rounds = rounds_of(count)
    slots = slots_of(count)

    def device(offset):
        t = lax.rem(me + offset + count, count)
        return (t // subs, lax.rem(t, subs))

    partners = sorted({o % count for _, o in slots} | {(-o) % count for _, o in slots})
    barrier = pltpu.get_barrier_semaphore()
    for p in partners:
        pl.semaphore_signal(barrier, inc=1, device_id=device(p), device_id_type=MESH)

    first_fringe = count * stations - FRINGE_STATIONS
    damp = jnp.float32(fringe_total ** (1.0 / FRINGE_STATIONS))
    for copy in copies:
        copy.wait()

    def step(i, carry):
        pr, pi, xr, xi = carry
        r = station(rbuf, i, fields, stations)
        ph = station(pbuf, i, fields, stations)
        sponge = jnp.where(me * stations + i >= first_fringe, damp, jnp.float32(1.0))
        mag = jnp.exp(-r) * sponge
        cr = mag * jnp.cos(ph)
        ci = mag * jnp.sin(ph)
        sc = jnp.sqrt(-expm1(-2.0 * r))
        coef_ref[0, i] = cr
        coef_ref[1, i] = ci
        coef_ref[2, i] = sc
        npr = cr * pr - ci * pi
        npi = cr * pi + ci * pr
        nxr, nxi = [], []
        for e in range(ex):
            fr = station(fbuf.at[e], i, fields, stations)
            fi = station(fbuf.at[ex + e], i, fields, stations)
            nxr.append(cr * xr[e] - ci * xi[e] + sc * fr)
            nxi.append(cr * xi[e] + ci * xr[e] + sc * fi)
        return npr, npi, tuple(nxr), tuple(nxi)

    shape = (fields, wall)
    one = jnp.ones(shape, jnp.float32)
    zero = jnp.zeros(shape, jnp.float32)
    init = (one, zero, (zero,) * ex, (zero,) * ex)
    pr, pi, xr, xi = lax.fori_loop(0, stations, step, init, unroll=4)

    values = [(xr[e], xi[e]) for e in range(ex)] + [(pr, pi)]
    for j, pair in enumerate(values):
        for c in range(2):
            tmp[...] = pair[c]
            for f in range(fields):
                for q in range(chunks):
                    pack[c, j, pl.ds(f * chunks + q, 1), :] = tmp[
                        pl.ds(f, 1), pl.ds(q * LANES, LANES)
                    ]

    pl.semaphore_wait(barrier, len(partners))

    def put(buf, n, i, value):
        rows = pl.ds(i, fields, stride=stations)
        for q in range(chunks):
            buf[n, q, rows, :] = value[:, q * LANES:(q + 1) * LANES]

    def local_march():
        def step(i, carry):
            pr, pi, xr, xi = carry
            cr = coef_ref[0, i]
            ci = coef_ref[1, i]
            sc = coef_ref[2, i]
            npr = cr * pr - ci * pi
            npi = cr * pi + ci * pr
            put(gbuf, 0, i, npr)
            put(gbuf, 1, i, npi)
            nxr, nxi = [], []
            for e in range(ex):
                fr = station(fbuf.at[e], i, fields, stations)
                fi = station(fbuf.at[ex + e], i, fields, stations)
                r = cr * xr[e] - ci * xi[e] + sc * fr
                m = cr * xi[e] + ci * xr[e] + sc * fi
                put(qbuf, e, i, r)
                put(qbuf, ex + e, i, m)
                nxr.append(r)
                nxi.append(m)
            return npr, npi, tuple(nxr), tuple(nxi)

        lax.fori_loop(0, stations, step, init, unroll=4)
        sends = []
        for n in range(2 * ex + 2):
            for q in range(chunks):
                lanes = pl.ds(q * LANES, LANES)
                if n < 2 * ex:
                    src, dst = qbuf.at[n, q], out_hbm.at[n, :, lanes]
                else:
                    src, dst = gbuf.at[n - 2 * ex, q], (gr_hbm, gi_hbm)[n - 2 * ex].at[:, lanes]
                copy = pltpu.make_async_copy(src, dst, out_sem.at[n * chunks + q])
                copy.start()
                sends.append(copy)
        return sends

    def load(ref):
        return [(ref[0, j], ref[1, j]) for j in range(ex + 1)]

    def compose(earlier, later):
        ar, ai = later[ex]
        out = []
        for j in range(ex + 1):
            br, bi = earlier[j]
            nr = ar * br - ai * bi
            ni = ar * bi + ai * br
            if j < ex:
                nr = nr + later[j][0]
                ni = ni + later[j][1]
            out.append((nr, ni))
        return out

    held = None
    for k in range(len(rounds)):
        mine = [i for i, (r, _) in enumerate(slots) if r == k]
        src = pack if k == 0 else cur.at[k]
        copies = []
        for i in mine:
            copy = pltpu.make_async_remote_copy(
                src_ref=src,
                dst_ref=recv.at[i],
                send_sem=send_sem.at[i],
                recv_sem=recv_sem.at[i],
                device_id=device(slots[i][1]),
                device_id_type=MESH,
            )
            copy.start()
            copies.append(copy)
        if k == 0:
            stored = local_march()
        for n, (i, copy) in enumerate(zip(mine, copies)):
            copy.wait()
            arrived = load(recv.at[i])
            held = arrived if (k == 0 and n == 0) else compose(arrived, held)
        if k + 1 < len(rounds):
            dst = cur.at[k + 1]
            for j, (nr, ni) in enumerate(held):
                dst[0, j] = nr
                dst[1, j] = ni
            held = load(dst)

    gr, gi = held[ex]
    denom_re = 1.0 - gr
    denom_im = -gi
    size = denom_re * denom_re + denom_im * denom_im
    ent = cur.at[0]
    for j in range(ex):
        br, bi = held[j]
        ent[0, j] = (br * denom_re + bi * denom_im) / size
        ent[1, j] = (bi * denom_re - br * denom_im) / size
    for c in range(2):
        for e in range(ex):
            for f in range(fields):
                for q in range(chunks):
                    x0_ref[c, e, pl.ds(f, 1), pl.ds(q * LANES, LANES)] = ent[
                        c, e, pl.ds(f * chunks + q, 1), :
                    ]
    x0_ref[2] = -x0_ref[1]
    x0_ref[3] = x0_ref[0]

    for copy in stored:
        copy.wait()


def local(rate, phase, forcing):
    stations, fields, wall = rate.shape
    two, ex = forcing.shape[:2]
    count = lax.axis_size(AXES)
    subs = lax.axis_size("sub")
    rate_t = jnp.transpose(rate, (1, 0, 2)).reshape(fields * stations, wall)
    phase_t = jnp.transpose(phase, (1, 0, 2)).reshape(fields * stations, wall)
    forcing_t = jnp.transpose(forcing, (0, 1, 3, 2, 4)).reshape(
        two * ex, fields * stations, wall
    )
    n_slots = len(slots_of(count))
    n_rounds = len(rounds_of(count))
    packed = (2, ex + 1, fields * wall // LANES, LANES)
    vmem = pl.BlockSpec(memory_space=pltpu.VMEM)
    hbm = pl.BlockSpec(memory_space=pl.ANY)
    chunks = wall // LANES
    slab = (fields * stations, LANES)
    fbuf = pltpu.VMEM((two * ex, chunks) + slab, jnp.float32)
    blocks = two * ex + 2
    offset, gain_r, gain_i, x0 = pl.pallas_call(
        functools.partial(resolvent_kernel, count, subs),
        out_shape=(
            jax.ShapeDtypeStruct(forcing_t.shape, jnp.float32),
            jax.ShapeDtypeStruct(forcing_t.shape[1:], jnp.float32),
            jax.ShapeDtypeStruct(forcing_t.shape[1:], jnp.float32),
            jax.ShapeDtypeStruct((4, ex, fields, wall), jnp.float32),
        ),
        in_specs=[hbm] * 3,
        out_specs=(hbm, hbm, hbm, vmem),
        scratch_shapes=[
            pltpu.VMEM((chunks,) + slab, jnp.float32),
            pltpu.VMEM((chunks,) + slab, jnp.float32),
            fbuf,
            pltpu.SemaphoreType.DMA(((2 + two * ex) * chunks,)),
            pltpu.VMEM((3, stations, fields, wall), jnp.float32),
            fbuf,
            pltpu.VMEM((2, chunks) + slab, jnp.float32),
            pltpu.SemaphoreType.DMA((blocks * chunks,)),
            pltpu.VMEM((fields, wall), jnp.float32),
            pltpu.VMEM(packed, jnp.float32),
            pltpu.VMEM((n_slots,) + packed, jnp.float32),
            pltpu.VMEM((n_rounds,) + packed, jnp.float32),
            pltpu.SemaphoreType.DMA((n_slots,)),
            pltpu.SemaphoreType.DMA((n_slots,)),
        ],
        compiler_params=pltpu.CompilerParams(collective_id=0, has_side_effects=True),
    )(rate_t, phase_t, forcing_t)
    x0 = x0.reshape(2, 2, ex, fields, 1, wall)
    out_t = (
        offset.reshape(two, ex, fields, stations, wall)
        + gain_r.reshape(fields, stations, wall) * x0[0]
        + gain_i.reshape(fields, stations, wall) * x0[1]
    )
    return jnp.transpose(out_t, (0, 1, 3, 2, 4))


def solution(mesh):
    count = mesh.shape["loop"] * mesh.shape["sub"]
    assert count & (count - 1) == 0
    placed = (
        P(AXES, None, None),
        P(AXES, None, None),
        P(None, None, AXES, None, None),
    )
    return jax.shard_map(
        local,
        mesh=mesh,
        in_specs=placed,
        out_specs=P(None, None, AXES, None, None),
        check_vma=False,
    )
```

```python
import functools

import jax
import jax.numpy as jnp
from jax import lax
from jax.experimental import pallas as pl
from jax.experimental.pallas import tpu as pltpu
from jax.sharding import PartitionSpec as P

fringe_total = 0.7
FRINGE_STATIONS = 32
AXES = ("loop", "sub")
MESH = pl.DeviceIdType.MESH
LANES = 128


def rounds_of(count):
    out, reach = [], 1
    while reach < count:
        fan = 4 if count % (reach * 4) == 0 else 2
        out.append((reach, fan))
        reach *= fan
    return out


def slots_of(count):
    slots = []
    for k, (stride, fan) in enumerate(rounds_of(count)):
        for j in range(1, fan + (1 if k == 0 else 0)):
            slots.append((k, j * stride))
    return slots


def expm1(x):
    u = jnp.exp(x)
    return jnp.where(u == 1.0, x, (u - 1.0) * x / jnp.log(u))


def fetch(srcs, bufs, sems):
    copies = []
    for n, (src, buf) in enumerate(zip(srcs, bufs)):
        for q in range(buf.shape[0]):
            copy = pltpu.make_async_copy(
                src.at[:, pl.ds(q * LANES, LANES)], buf.at[q], sems.at[n * buf.shape[0] + q]
            )
            copy.start()
            copies.append(copy)
    return copies


def station(buf, i, fields, stations):
    rows = pl.ds(i, fields, stride=stations)
    return jnp.concatenate([buf[q, rows, :] for q in range(buf.shape[0])], axis=1)


def resolvent_kernel(count, subs, rate_hbm, phase_hbm, f_hbm, out_hbm,
                     rbuf, pbuf, fbuf, in_sem, coef_ref, x0_ref, qbuf, gbuf, out_sem,
                     tmp, pack, recv, cur, send_sem, recv_sem):
    ex = x0_ref.shape[1]
    fields, wall = x0_ref.shape[2:]
    chunks = wall // LANES
    stations = rbuf.shape[1] // fields
    copies = fetch(
        [rate_hbm, phase_hbm] + [f_hbm.at[n] for n in range(2 * ex)],
        [rbuf, pbuf] + [fbuf.at[n] for n in range(2 * ex)],
        in_sem,
    )
    me = lax.axis_index("loop") * subs + lax.axis_index("sub")
    rounds = rounds_of(count)
    slots = slots_of(count)

    def device(offset):
        t = lax.rem(me + offset + count, count)
        return (t // subs, lax.rem(t, subs))

    partners = sorted({o % count for _, o in slots} | {(-o) % count for _, o in slots})
    barrier = pltpu.get_barrier_semaphore()
    for p in partners:
        pl.semaphore_signal(barrier, inc=1, device_id=device(p), device_id_type=MESH)

    first_fringe = count * stations - FRINGE_STATIONS
    damp = jnp.float32(fringe_total ** (1.0 / FRINGE_STATIONS))
    for copy in copies:
        copy.wait()

    station_of_row = lax.broadcasted_iota(jnp.int32, rbuf.shape[1:], 0) % stations
    sponge = jnp.where(me * stations + station_of_row >= first_fringe, damp, jnp.float32(1.0))
    for q in range(chunks):
        r = rbuf[q]
        ph = pbuf[q]
        mag = jnp.exp(-r) * sponge
        coef_ref[0, q] = mag * jnp.cos(ph)
        coef_ref[1, q] = mag * jnp.sin(ph)
        coef_ref[2, q] = jnp.sqrt(-expm1(-2.0 * r))

    def step(i, carry):
        pr, pi, xr, xi = carry
        cr = station(coef_ref.at[0], i, fields, stations)
        ci = station(coef_ref.at[1], i, fields, stations)
        sc = station(coef_ref.at[2], i, fields, stations)
        npr = cr * pr - ci * pi
        npi = cr * pi + ci * pr
        nxr, nxi = [], []
        for e in range(ex):
            fr = station(fbuf.at[e], i, fields, stations)
            fi = station(fbuf.at[ex + e], i, fields, stations)
            nxr.append(cr * xr[e] - ci * xi[e] + sc * fr)
            nxi.append(cr * xi[e] + ci * xr[e] + sc * fi)
        return npr, npi, tuple(nxr), tuple(nxi)

    shape = (fields, wall)
    one = jnp.ones(shape, jnp.float32)
    zero = jnp.zeros(shape, jnp.float32)
    init = (one, zero, (zero,) * ex, (zero,) * ex)
    pr, pi, xr, xi = lax.fori_loop(0, stations, step, init, unroll=4)

    values = [(xr[e], xi[e]) for e in range(ex)] + [(pr, pi)]
    for j, pair in enumerate(values):
        for c in range(2):
            tmp[...] = pair[c]
            for f in range(fields):
                for q in range(chunks):
                    pack[c, j, pl.ds(f * chunks + q, 1), :] = tmp[
                        pl.ds(f, 1), pl.ds(q * LANES, LANES)
                    ]

    pl.semaphore_wait(barrier, len(partners))

    def put(buf, n, i, value):
        rows = pl.ds(i, fields, stride=stations)
        for q in range(chunks):
            buf[n, q, rows, :] = value[:, q * LANES:(q + 1) * LANES]

    def local_march():
        def step(i, carry):
            pr, pi, xr, xi = carry
            cr = station(coef_ref.at[0], i, fields, stations)
            ci = station(coef_ref.at[1], i, fields, stations)
            sc = station(coef_ref.at[2], i, fields, stations)
            npr = cr * pr - ci * pi
            npi = cr * pi + ci * pr
            put(gbuf, 0, i, npr)
            put(gbuf, 1, i, npi)
            nxr, nxi = [], []
            for e in range(ex):
                fr = station(fbuf.at[e], i, fields, stations)
                fi = station(fbuf.at[ex + e], i, fields, stations)
                r = cr * xr[e] - ci * xi[e] + sc * fr
                m = cr * xi[e] + ci * xr[e] + sc * fi
                put(qbuf, e, i, r)
                put(qbuf, ex + e, i, m)
                nxr.append(r)
                nxi.append(m)
            return npr, npi, tuple(nxr), tuple(nxi)

        lax.fori_loop(0, stations, step, init, unroll=4)

    def load(ref):
        return [(ref[0, j], ref[1, j]) for j in range(ex + 1)]

    def compose(earlier, later):
        ar, ai = later[ex]
        out = []
        for j in range(ex + 1):
            br, bi = earlier[j]
            nr = ar * br - ai * bi
            ni = ar * bi + ai * br
            if j < ex:
                nr = nr + later[j][0]
                ni = ni + later[j][1]
            out.append((nr, ni))
        return out

    held = None
    for k in range(len(rounds)):
        mine = [i for i, (r, _) in enumerate(slots) if r == k]
        src = pack if k == 0 else cur.at[k]
        copies = []
        for i in mine:
            copy = pltpu.make_async_remote_copy(
                src_ref=src,
                dst_ref=recv.at[i],
                send_sem=send_sem.at[i],
                recv_sem=recv_sem.at[i],
                device_id=device(slots[i][1]),
                device_id_type=MESH,
            )
            copy.start()
            copies.append(copy)
        if k == 0:
            local_march()
        for n, (i, copy) in enumerate(zip(mine, copies)):
            copy.wait()
            arrived = load(recv.at[i])
            held = arrived if (k == 0 and n == 0) else compose(arrived, held)
        if k + 1 < len(rounds):
            dst = cur.at[k + 1]
            for j, (nr, ni) in enumerate(held):
                dst[0, j] = nr
                dst[1, j] = ni
            held = load(dst)

    gr, gi = held[ex]
    denom_re = 1.0 - gr
    denom_im = -gi
    size = denom_re * denom_re + denom_im * denom_im
    ent = cur.at[0]
    for j in range(ex):
        br, bi = held[j]
        ent[0, j] = (br * denom_re + bi * denom_im) / size
        ent[1, j] = (bi * denom_re - br * denom_im) / size
    for c in range(2):
        for e in range(ex):
            for f in range(fields):
                for q in range(chunks):
                    x0_ref[c, e, pl.ds(f, 1), pl.ds(q * LANES, LANES)] = ent[
                        c, e, pl.ds(f * chunks + q, 1), :
                    ]

    copies = []
    for e in range(ex):
        for q in range(chunks):
            lanes = pl.ds(q * LANES, LANES)
            for f in range(fields):
                rows = pl.ds(f * stations, stations)
                xr = x0_ref[0, e, pl.ds(f, 1), lanes]
                xi = x0_ref[1, e, pl.ds(f, 1), lanes]
                gr = gbuf[0, q, rows, :]
                gi = gbuf[1, q, rows, :]
                qbuf[e, q, rows, :] = qbuf[e, q, rows, :] + (gr * xr - gi * xi)
                qbuf[ex + e, q, rows, :] = qbuf[ex + e, q, rows, :] + (gr * xi + gi * xr)
            for n in (e, ex + e):
                copy = pltpu.make_async_copy(
                    qbuf.at[n, q], out_hbm.at[n, :, lanes], out_sem.at[n * chunks + q]
                )
                copy.start()
                copies.append(copy)
    for copy in copies:
        copy.wait()


def local(rate, phase, forcing):
    stations, fields, wall = rate.shape
    two, ex = forcing.shape[:2]
    count = lax.axis_size(AXES)
    subs = lax.axis_size("sub")
    rate_t = jnp.transpose(rate, (1, 0, 2)).reshape(fields * stations, wall)
    phase_t = jnp.transpose(phase, (1, 0, 2)).reshape(fields * stations, wall)
    forcing_t = jnp.transpose(forcing, (0, 1, 3, 2, 4)).reshape(
        two * ex, fields * stations, wall
    )
    n_slots = len(slots_of(count))
    n_rounds = len(rounds_of(count))
    packed = (2, ex + 1, fields * wall // LANES, LANES)
    vmem = pl.BlockSpec(memory_space=pltpu.VMEM)
    hbm = pl.BlockSpec(memory_space=pl.ANY)
    chunks = wall // LANES
    slab = (fields * stations, LANES)
    fbuf = pltpu.VMEM((two * ex, chunks) + slab, jnp.float32)
    out_t = pl.pallas_call(
        functools.partial(resolvent_kernel, count, subs),
        out_shape=jax.ShapeDtypeStruct(forcing_t.shape, jnp.float32),
        in_specs=[hbm] * 3,
        out_specs=hbm,
        scratch_shapes=[
            pltpu.VMEM((chunks,) + slab, jnp.float32),
            pltpu.VMEM((chunks,) + slab, jnp.float32),
            fbuf,
            pltpu.SemaphoreType.DMA(((2 + two * ex) * chunks,)),
            pltpu.VMEM((3, chunks) + slab, jnp.float32),
            pltpu.VMEM((2, ex, fields, wall), jnp.float32),
            fbuf,
            pltpu.VMEM((2, chunks) + slab, jnp.float32),
            pltpu.SemaphoreType.DMA((two * ex * chunks,)),
            pltpu.VMEM((fields, wall), jnp.float32),
            pltpu.VMEM(packed, jnp.float32),
            pltpu.VMEM((n_slots,) + packed, jnp.float32),
            pltpu.VMEM((n_rounds,) + packed, jnp.float32),
            pltpu.SemaphoreType.DMA((n_slots,)),
            pltpu.SemaphoreType.DMA((n_slots,)),
        ],
        compiler_params=pltpu.CompilerParams(collective_id=0, has_side_effects=True),
    )(rate_t, phase_t, forcing_t)
    return jnp.transpose(out_t.reshape(two, ex, fields, stations, wall), (0, 1, 3, 2, 4))


def solution(mesh):
    count = mesh.shape["loop"] * mesh.shape["sub"]
    assert count & (count - 1) == 0
    placed = (
        P(AXES, None, None),
        P(AXES, None, None),
        P(None, None, AXES, None, None),
    )
    return jax.shard_map(
        local,
        mesh=mesh,
        in_specs=placed,
        out_specs=P(None, None, AXES, None, None),
        check_vma=False,
    )
```

```python
import functools

import jax
import jax.numpy as jnp
from jax import lax
from jax.experimental import pallas as pl
from jax.experimental.pallas import tpu as pltpu
from jax.sharding import PartitionSpec as P

fringe_total = 0.7
FRINGE_STATIONS = 32
AXES = ("loop", "sub")
MESH = pl.DeviceIdType.MESH
LANES = 128


def rounds_of(count):
    out, reach = [], 1
    while reach < count:
        fan = 4 if count % (reach * 4) == 0 else 2
        out.append((reach, fan))
        reach *= fan
    return out


def slots_of(count):
    slots = []
    for k, (stride, fan) in enumerate(rounds_of(count)):
        for j in range(1, fan + (1 if k == 0 else 0)):
            slots.append((k, j * stride))
    return slots


def expm1(x):
    u = jnp.exp(x)
    return jnp.where(u == 1.0, x, (u - 1.0) * x / jnp.log(u))


def fetch(srcs, bufs, sems):
    copies = []
    for n, (src, buf) in enumerate(zip(srcs, bufs)):
        for q in range(buf.shape[0]):
            copy = pltpu.make_async_copy(
                src.at[:, pl.ds(q * LANES, LANES)], buf.at[q], sems.at[n * buf.shape[0] + q]
            )
            copy.start()
            copies.append(copy)
    return copies


def station(buf, i, fields, stations):
    rows = pl.ds(i, fields, stride=stations)
    return jnp.concatenate([buf[q, rows, :] for q in range(buf.shape[0])], axis=1)


def resolvent_kernel(count, subs, rate_hbm, phase_hbm, f_hbm, out_hbm,
                     rbuf, pbuf, fbuf, in_sem, coef_ref, x0_ref, qbuf, gbuf, out_sem,
                     tmp, pack, recv, cur, send_sem, recv_sem):
    ex = x0_ref.shape[1]
    stations, fields, wall = coef_ref.shape[1:]
    chunks = wall // LANES
    copies = fetch(
        [rate_hbm, phase_hbm] + [f_hbm.at[n] for n in range(2 * ex)],
        [rbuf, pbuf] + [fbuf.at[n] for n in range(2 * ex)],
        in_sem,
    )
    me = lax.axis_index("loop") * subs + lax.axis_index("sub")
    rounds = rounds_of(count)
    slots = slots_of(count)

    def device(offset):
        t = lax.rem(me + offset + count, count)
        return (t // subs, lax.rem(t, subs))

    partners = sorted({o % count for _, o in slots} | {(-o) % count for _, o in slots})
    barrier = pltpu.get_barrier_semaphore()
    for p in partners:
        pl.semaphore_signal(barrier, inc=1, device_id=device(p), device_id_type=MESH)

    first_fringe = count * stations - FRINGE_STATIONS
    damp = jnp.float32(fringe_total ** (1.0 / FRINGE_STATIONS))
    for copy in copies:
        copy.wait()

    def step(i, carry):
        pr, pi, xr, xi = carry
        r = station(rbuf, i, fields, stations)
        ph = station(pbuf, i, fields, stations)
        sponge = jnp.where(me * stations + i >= first_fringe, damp, jnp.float32(1.0))
        mag = jnp.exp(-r) * sponge
        cr = mag * jnp.cos(ph)
        ci = mag * jnp.sin(ph)
        sc = jnp.sqrt(-expm1(-2.0 * r))
        coef_ref[0, i] = cr
        coef_ref[1, i] = ci
        coef_ref[2, i] = sc
        npr = cr * pr - ci * pi
        npi = cr * pi + ci * pr
        nxr, nxi = [], []
        for e in range(ex):
            fr = station(fbuf.at[e], i, fields, stations)
            fi = station(fbuf.at[ex + e], i, fields, stations)
            nxr.append(cr * xr[e] - ci * xi[e] + sc * fr)
            nxi.append(cr * xi[e] + ci * xr[e] + sc * fi)
        return npr, npi, tuple(nxr), tuple(nxi)

    shape = (fields, wall)
    one = jnp.ones(shape, jnp.float32)
    zero = jnp.zeros(shape, jnp.float32)
    init = (one, zero, (zero,) * ex, (zero,) * ex)
    pr, pi, xr, xi = lax.fori_loop(0, stations, step, init, unroll=8)

    values = [(xr[e], xi[e]) for e in range(ex)] + [(pr, pi)]
    for j, pair in enumerate(values):
        for c in range(2):
            tmp[...] = pair[c]
            for f in range(fields):
                for q in range(chunks):
                    pack[c, j, pl.ds(f * chunks + q, 1), :] = tmp[
                        pl.ds(f, 1), pl.ds(q * LANES, LANES)
                    ]

    pl.semaphore_wait(barrier, len(partners))

    def put(buf, n, i, value):
        rows = pl.ds(i, fields, stride=stations)
        for q in range(chunks):
            buf[n, q, rows, :] = value[:, q * LANES:(q + 1) * LANES]

    def local_march():
        def step(i, carry):
            pr, pi, xr, xi = carry
            cr = coef_ref[0, i]
            ci = coef_ref[1, i]
            sc = coef_ref[2, i]
            npr = cr * pr - ci * pi
            npi = cr * pi + ci * pr
            put(gbuf, 0, i, npr)
            put(gbuf, 1, i, npi)
            nxr, nxi = [], []
            for e in range(ex):
                fr = station(fbuf.at[e], i, fields, stations)
                fi = station(fbuf.at[ex + e], i, fields, stations)
                r = cr * xr[e] - ci * xi[e] + sc * fr
                m = cr * xi[e] + ci * xr[e] + sc * fi
                put(qbuf, e, i, r)
                put(qbuf, ex + e, i, m)
                nxr.append(r)
                nxi.append(m)
            return npr, npi, tuple(nxr), tuple(nxi)

        lax.fori_loop(0, stations, step, init, unroll=4)

    def load(ref):
        return [(ref[0, j], ref[1, j]) for j in range(ex + 1)]

    def compose(earlier, later):
        ar, ai = later[ex]
        out = []
        for j in range(ex + 1):
            br, bi = earlier[j]
            nr = ar * br - ai * bi
            ni = ar * bi + ai * br
            if j < ex:
                nr = nr + later[j][0]
                ni = ni + later[j][1]
            out.append((nr, ni))
        return out

    held = None
    for k in range(len(rounds)):
        mine = [i for i, (r, _) in enumerate(slots) if r == k]
        src = pack if k == 0 else cur.at[k]
        copies = []
        for i in mine:
            copy = pltpu.make_async_remote_copy(
                src_ref=src,
                dst_ref=recv.at[i],
                send_sem=send_sem.at[i],
                recv_sem=recv_sem.at[i],
                device_id=device(slots[i][1]),
                device_id_type=MESH,
            )
            copy.start()
            copies.append(copy)
        if k == 0:
            local_march()
        for n, (i, copy) in enumerate(zip(mine, copies)):
            copy.wait()
            arrived = load(recv.at[i])
            held = arrived if (k == 0 and n == 0) else compose(arrived, held)
        if k + 1 < len(rounds):
            dst = cur.at[k + 1]
            for j, (nr, ni) in enumerate(held):
                dst[0, j] = nr
                dst[1, j] = ni
            held = load(dst)

    gr, gi = held[ex]
    denom_re = 1.0 - gr
    denom_im = -gi
    size = denom_re * denom_re + denom_im * denom_im
    ent = cur.at[0]
    for j in range(ex):
        br, bi = held[j]
        ent[0, j] = (br * denom_re + bi * denom_im) / size
        ent[1, j] = (bi * denom_re - br * denom_im) / size
    for c in range(2):
        for e in range(ex):
            for f in range(fields):
                for q in range(chunks):
                    x0_ref[c, e, pl.ds(f, 1), pl.ds(q * LANES, LANES)] = ent[
                        c, e, pl.ds(f * chunks + q, 1), :
                    ]

    copies = []
    for e in range(ex):
        for q in range(chunks):
            lanes = pl.ds(q * LANES, LANES)
            for f in range(fields):
                rows = pl.ds(f * stations, stations)
                xr = x0_ref[0, e, pl.ds(f, 1), lanes]
                xi = x0_ref[1, e, pl.ds(f, 1), lanes]
                gr = gbuf[0, q, rows, :]
                gi = gbuf[1, q, rows, :]
                qbuf[e, q, rows, :] = qbuf[e, q, rows, :] + (gr * xr - gi * xi)
                qbuf[ex + e, q, rows, :] = qbuf[ex + e, q, rows, :] + (gr * xi + gi * xr)
            for n in (e, ex + e):
                copy = pltpu.make_async_copy(
                    qbuf.at[n, q], out_hbm.at[n, :, lanes], out_sem.at[n * chunks + q]
                )
                copy.start()
                copies.append(copy)
    for copy in copies:
        copy.wait()


def local(rate, phase, forcing):
    stations, fields, wall = rate.shape
    two, ex = forcing.shape[:2]
    count = lax.axis_size(AXES)
    subs = lax.axis_size("sub")
    rate_t = jnp.transpose(rate, (1, 0, 2)).reshape(fields * stations, wall)
    phase_t = jnp.transpose(phase, (1, 0, 2)).reshape(fields * stations, wall)
    forcing_t = jnp.transpose(forcing, (0, 1, 3, 2, 4)).reshape(
        two * ex, fields * stations, wall
    )
    n_slots = len(slots_of(count))
    n_rounds = len(rounds_of(count))
    packed = (2, ex + 1, fields * wall // LANES, LANES)
    vmem = pl.BlockSpec(memory_space=pltpu.VMEM)
    hbm = pl.BlockSpec(memory_space=pl.ANY)
    chunks = wall // LANES
    slab = (fields * stations, LANES)
    fbuf = pltpu.VMEM((two * ex, chunks) + slab, jnp.float32)
    out_t = pl.pallas_call(
        functools.partial(resolvent_kernel, count, subs),
        out_shape=jax.ShapeDtypeStruct(forcing_t.shape, jnp.float32),
        in_specs=[hbm] * 3,
        out_specs=hbm,
        scratch_shapes=[
            pltpu.VMEM((chunks,) + slab, jnp.float32),
            pltpu.VMEM((chunks,) + slab, jnp.float32),
            fbuf,
            pltpu.SemaphoreType.DMA(((2 + two * ex) * chunks,)),
            pltpu.VMEM((3, stations, fields, wall), jnp.float32),
            pltpu.VMEM((2, ex, fields, wall), jnp.float32),
            fbuf,
            pltpu.VMEM((2, chunks) + slab, jnp.float32),
            pltpu.SemaphoreType.DMA((two * ex * chunks,)),
            pltpu.VMEM((fields, wall), jnp.float32),
            pltpu.VMEM(packed, jnp.float32),
            pltpu.VMEM((n_slots,) + packed, jnp.float32),
            pltpu.VMEM((n_rounds,) + packed, jnp.float32),
            pltpu.SemaphoreType.DMA((n_slots,)),
            pltpu.SemaphoreType.DMA((n_slots,)),
        ],
        compiler_params=pltpu.CompilerParams(collective_id=0, has_side_effects=True),
    )(rate_t, phase_t, forcing_t)
    return jnp.transpose(out_t.reshape(two, ex, fields, stations, wall), (0, 1, 3, 2, 4))


def solution(mesh):
    count = mesh.shape["loop"] * mesh.shape["sub"]
    assert count & (count - 1) == 0
    placed = (
        P(AXES, None, None),
        P(AXES, None, None),
        P(None, None, AXES, None, None),
    )
    return jax.shard_map(
        local,
        mesh=mesh,
        in_specs=placed,
        out_specs=P(None, None, AXES, None, None),
        check_vma=False,
    )
```

```python
import functools

import jax
import jax.numpy as jnp
from jax import lax
from jax.experimental import pallas as pl
from jax.experimental.pallas import tpu as pltpu
from jax.sharding import PartitionSpec as P

fringe_total = 0.7
FRINGE_STATIONS = 32
AXES = ("loop", "sub")
MESH = pl.DeviceIdType.MESH
LANES = 128


def rounds_of(count):
    out, reach = [], 1
    while reach < count:
        fan = 4 if count % (reach * 4) == 0 else 2
        out.append((reach, fan))
        reach *= fan
    return out


def slots_of(count):
    slots = []
    for k, (stride, fan) in enumerate(rounds_of(count)):
        for j in range(1, fan + (1 if k == 0 else 0)):
            slots.append((k, j * stride))
    return slots


def expm1(x):
    u = jnp.exp(x)
    return jnp.where(u == 1.0, x, (u - 1.0) * x / jnp.log(u))


def fetch(srcs, bufs, sems):
    copies = []
    for n, (src, buf) in enumerate(zip(srcs, bufs)):
        for q in range(buf.shape[0]):
            copy = pltpu.make_async_copy(
                src.at[:, pl.ds(q * LANES, LANES)], buf.at[q], sems.at[n * buf.shape[0] + q]
            )
            copy.start()
            copies.append(copy)
    return copies


def station(buf, i, fields, stations):
    rows = pl.ds(i, fields, stride=stations)
    return jnp.concatenate([buf[q, rows, :] for q in range(buf.shape[0])], axis=1)


def resolvent_kernel(count, subs, rate_hbm, phase_hbm, f_hbm, out_hbm,
                     rbuf, pbuf, fbuf, in_sem, coef_ref, x0_ref, qbuf, gbuf, out_sem,
                     tmp, pack, recv, cur, send_sem, recv_sem):
    ex = x0_ref.shape[1]
    stations, fields, wall = coef_ref.shape[1:]
    chunks = wall // LANES
    copies = fetch(
        [rate_hbm, phase_hbm] + [f_hbm.at[n] for n in range(2 * ex)],
        [rbuf, pbuf] + [fbuf.at[n] for n in range(2 * ex)],
        in_sem,
    )
    me = lax.axis_index("loop") * subs + lax.axis_index("sub")
    rounds = rounds_of(count)
    slots = slots_of(count)

    def device(offset):
        t = lax.rem(me + offset + count, count)
        return (t // subs, lax.rem(t, subs))

    partners = sorted({o % count for _, o in slots} | {(-o) % count for _, o in slots})
    barrier = pltpu.get_barrier_semaphore()
    for p in partners:
        pl.semaphore_signal(barrier, inc=1, device_id=device(p), device_id_type=MESH)

    first_fringe = count * stations - FRINGE_STATIONS
    damp = jnp.float32(fringe_total ** (1.0 / FRINGE_STATIONS))
    for copy in copies:
        copy.wait()

    def step(i, carry):
        pr, pi, xr, xi = carry
        r = station(rbuf, i, fields, stations)
        ph = station(pbuf, i, fields, stations)
        sponge = jnp.where(me * stations + i >= first_fringe, damp, jnp.float32(1.0))
        mag = jnp.exp(-r) * sponge
        cr = mag * jnp.cos(ph)
        ci = mag * jnp.sin(ph)
        sc = jnp.sqrt(-expm1(-2.0 * r))
        coef_ref[0, i] = cr
        coef_ref[1, i] = ci
        coef_ref[2, i] = sc
        npr = cr * pr - ci * pi
        npi = cr * pi + ci * pr
        nxr, nxi = [], []
        for e in range(ex):
            fr = station(fbuf.at[e], i, fields, stations)
            fi = station(fbuf.at[ex + e], i, fields, stations)
            nxr.append(cr * xr[e] - ci * xi[e] + sc * fr)
            nxi.append(cr * xi[e] + ci * xr[e] + sc * fi)
        return npr, npi, tuple(nxr), tuple(nxi)

    shape = (fields, wall)
    one = jnp.ones(shape, jnp.float32)
    zero = jnp.zeros(shape, jnp.float32)
    init = (one, zero, (zero,) * ex, (zero,) * ex)
    pr, pi, xr, xi = lax.fori_loop(0, stations, step, init, unroll=4)

    rows_per = fields * chunks

    def block(c, j):
        return pl.ds((c * (ex + 1) + j) * rows_per, rows_per)

    values = [(xr[e], xi[e]) for e in range(ex)] + [(pr, pi)]
    for j, pair in enumerate(values):
        for c in range(2):
            tmp[...] = pair[c]
            for f in range(fields):
                for q in range(chunks):
                    pack[pl.ds((c * (ex + 1) + j) * rows_per + f * chunks + q, 1), :] = tmp[
                        pl.ds(f, 1), pl.ds(q * LANES, LANES)
                    ]

    pl.semaphore_wait(barrier, len(partners))

    def put(buf, n, i, value):
        rows = pl.ds(i, fields, stride=stations)
        for q in range(chunks):
            buf[n, q, rows, :] = value[:, q * LANES:(q + 1) * LANES]

    def local_march():
        def step(i, carry):
            pr, pi, xr, xi = carry
            cr = coef_ref[0, i]
            ci = coef_ref[1, i]
            sc = coef_ref[2, i]
            npr = cr * pr - ci * pi
            npi = cr * pi + ci * pr
            put(gbuf, 0, i, npr)
            put(gbuf, 1, i, npi)
            nxr, nxi = [], []
            for e in range(ex):
                fr = station(fbuf.at[e], i, fields, stations)
                fi = station(fbuf.at[ex + e], i, fields, stations)
                r = cr * xr[e] - ci * xi[e] + sc * fr
                m = cr * xi[e] + ci * xr[e] + sc * fi
                put(qbuf, e, i, r)
                put(qbuf, ex + e, i, m)
                nxr.append(r)
                nxi.append(m)
            return npr, npi, tuple(nxr), tuple(nxi)

        lax.fori_loop(0, stations, step, init, unroll=4)

    def load(ref):
        return [(ref[block(0, j), :], ref[block(1, j), :]) for j in range(ex + 1)]

    def compose(earlier, later):
        ar, ai = later[ex]
        out = []
        for j in range(ex + 1):
            br, bi = earlier[j]
            nr = ar * br - ai * bi
            ni = ar * bi + ai * br
            if j < ex:
                nr = nr + later[j][0]
                ni = ni + later[j][1]
            out.append((nr, ni))
        return out

    held = None
    for k in range(len(rounds)):
        mine = [i for i, (r, _) in enumerate(slots) if r == k]
        src = pack if k == 0 else cur.at[k]
        copies = []
        for i in mine:
            copy = pltpu.make_async_remote_copy(
                src_ref=src,
                dst_ref=recv.at[i],
                send_sem=send_sem.at[i],
                recv_sem=recv_sem.at[i],
                device_id=device(slots[i][1]),
                device_id_type=MESH,
            )
            copy.start()
            copies.append(copy)
        if k == 0:
            local_march()
        for n, (i, copy) in enumerate(zip(mine, copies)):
            copy.wait()
            arrived = load(recv.at[i])
            held = arrived if (k == 0 and n == 0) else compose(arrived, held)
        if k + 1 < len(rounds):
            dst = cur.at[k + 1]
            for j, (nr, ni) in enumerate(held):
                dst[block(0, j), :] = nr
                dst[block(1, j), :] = ni
            held = load(dst)

    gr, gi = held[ex]
    denom_re = 1.0 - gr
    denom_im = -gi
    size = denom_re * denom_re + denom_im * denom_im
    ent = cur.at[0]
    for j in range(ex):
        br, bi = held[j]
        ent[block(0, j), :] = (br * denom_re + bi * denom_im) / size
        ent[block(1, j), :] = (bi * denom_re - br * denom_im) / size
    for c in range(2):
        for e in range(ex):
            for f in range(fields):
                for q in range(chunks):
                    x0_ref[c, e, pl.ds(f, 1), pl.ds(q * LANES, LANES)] = ent[
                        pl.ds((c * (ex + 1) + e) * rows_per + f * chunks + q, 1), :
                    ]

    copies = []
    for e in range(ex):
        for q in range(chunks):
            lanes = pl.ds(q * LANES, LANES)
            for f in range(fields):
                rows = pl.ds(f * stations, stations)
                xr = x0_ref[0, e, pl.ds(f, 1), lanes]
                xi = x0_ref[1, e, pl.ds(f, 1), lanes]
                gr = gbuf[0, q, rows, :]
                gi = gbuf[1, q, rows, :]
                qbuf[e, q, rows, :] = qbuf[e, q, rows, :] + (gr * xr - gi * xi)
                qbuf[ex + e, q, rows, :] = qbuf[ex + e, q, rows, :] + (gr * xi + gi * xr)
            for n in (e, ex + e):
                copy = pltpu.make_async_copy(
                    qbuf.at[n, q], out_hbm.at[n, :, lanes], out_sem.at[n * chunks + q]
                )
                copy.start()
                copies.append(copy)
    for copy in copies:
        copy.wait()


def local(rate, phase, forcing):
    stations, fields, wall = rate.shape
    two, ex = forcing.shape[:2]
    count = lax.axis_size(AXES)
    subs = lax.axis_size("sub")
    rate_t = jnp.transpose(rate, (1, 0, 2)).reshape(fields * stations, wall)
    phase_t = jnp.transpose(phase, (1, 0, 2)).reshape(fields * stations, wall)
    forcing_t = jnp.transpose(forcing, (0, 1, 3, 2, 4)).reshape(
        two * ex, fields * stations, wall
    )
    n_slots = len(slots_of(count))
    n_rounds = len(rounds_of(count))
    packed = (2 * (ex + 1) * fields * wall // LANES, LANES)
    vmem = pl.BlockSpec(memory_space=pltpu.VMEM)
    hbm = pl.BlockSpec(memory_space=pl.ANY)
    chunks = wall // LANES
    slab = (fields * stations, LANES)
    fbuf = pltpu.VMEM((two * ex, chunks) + slab, jnp.float32)
    out_t = pl.pallas_call(
        functools.partial(resolvent_kernel, count, subs),
        out_shape=jax.ShapeDtypeStruct(forcing_t.shape, jnp.float32),
        in_specs=[hbm] * 3,
        out_specs=hbm,
        scratch_shapes=[
            pltpu.VMEM((chunks,) + slab, jnp.float32),
            pltpu.VMEM((chunks,) + slab, jnp.float32),
            fbuf,
            pltpu.SemaphoreType.DMA(((2 + two * ex) * chunks,)),
            pltpu.VMEM((3, stations, fields, wall), jnp.float32),
            pltpu.VMEM((2, ex, fields, wall), jnp.float32),
            fbuf,
            pltpu.VMEM((2, chunks) + slab, jnp.float32),
            pltpu.SemaphoreType.DMA((two * ex * chunks,)),
            pltpu.VMEM((fields, wall), jnp.float32),
            pltpu.VMEM(packed, jnp.float32),
            pltpu.VMEM((n_slots,) + packed, jnp.float32),
            pltpu.VMEM((n_rounds,) + packed, jnp.float32),
            pltpu.SemaphoreType.DMA((n_slots,)),
            pltpu.SemaphoreType.DMA((n_slots,)),
        ],
        compiler_params=pltpu.CompilerParams(collective_id=0, has_side_effects=True),
    )(rate_t, phase_t, forcing_t)
    return jnp.transpose(out_t.reshape(two, ex, fields, stations, wall), (0, 1, 3, 2, 4))


def solution(mesh):
    count = mesh.shape["loop"] * mesh.shape["sub"]
    assert count & (count - 1) == 0
    placed = (
        P(AXES, None, None),
        P(AXES, None, None),
        P(None, None, AXES, None, None),
    )
    return jax.shard_map(
        local,
        mesh=mesh,
        in_specs=placed,
        out_specs=P(None, None, AXES, None, None),
        check_vma=False,
    )
```

```python
import functools

import jax
import jax.numpy as jnp
from jax import lax
from jax.experimental import pallas as pl
from jax.experimental.pallas import tpu as pltpu
from jax.sharding import PartitionSpec as P

fringe_total = 0.7
FRINGE_STATIONS = 32
AXES = ("loop", "sub")
MESH = pl.DeviceIdType.MESH
LANES = 128


def rounds_of(count):
    out, reach = [], 1
    while reach < count:
        fan = 4 if count % (reach * 4) == 0 else 2
        out.append((reach, fan))
        reach *= fan
    return out


def slots_of(count):
    slots = []
    for k, (stride, fan) in enumerate(rounds_of(count)):
        for j in range(1, fan + (1 if k == 0 else 0)):
            slots.append((k, j * stride))
    return slots


def expm1(x):
    u = jnp.exp(x)
    return jnp.where(u == 1.0, x, (u - 1.0) * x / jnp.log(u))


def fetch(srcs, bufs, sems):
    copies = []
    for n, (src, buf) in enumerate(zip(srcs, bufs)):
        for q in range(buf.shape[0]):
            copy = pltpu.make_async_copy(
                src.at[:, pl.ds(q * LANES, LANES)], buf.at[q], sems.at[n * buf.shape[0] + q]
            )
            copy.start()
            copies.append(copy)
    return copies


def station(buf, i, fields, stations):
    rows = pl.ds(i, fields, stride=stations)
    return jnp.concatenate([buf[q, rows, :] for q in range(buf.shape[0])], axis=1)


def resolvent_kernel(count, subs, rate_hbm, phase_hbm, f_hbm, out_hbm,
                     rbuf, pbuf, fbuf, in_sem, coef_ref, x0_ref, qbuf, gbuf, out_sem,
                     tmp, pack, recv, cur, send_sem, recv_sem):
    ex = x0_ref.shape[1]
    stations, fields, wall = coef_ref.shape[1:]
    chunks = wall // LANES
    copies = fetch(
        [rate_hbm, phase_hbm] + [f_hbm.at[n] for n in range(2 * ex)],
        [rbuf, pbuf] + [fbuf.at[n] for n in range(2 * ex)],
        in_sem,
    )
    me = lax.axis_index("loop") * subs + lax.axis_index("sub")
    rounds = rounds_of(count)
    slots = slots_of(count)

    def device(offset):
        t = lax.rem(me + offset + count, count)
        return (t // subs, lax.rem(t, subs))

    partners = sorted({o % count for _, o in slots} | {(-o) % count for _, o in slots})
    barrier = pltpu.get_barrier_semaphore()
    for p in partners:
        pl.semaphore_signal(barrier, inc=1, device_id=device(p), device_id_type=MESH)

    first_fringe = count * stations - FRINGE_STATIONS
    damp = jnp.float32(fringe_total ** (1.0 / FRINGE_STATIONS))
    for copy in copies:
        copy.wait()

    def step(i, carry):
        pr, pi, xr, xi = carry
        r = station(rbuf, i, fields, stations)
        ph = station(pbuf, i, fields, stations)
        sponge = jnp.where(me * stations + i >= first_fringe, damp, jnp.float32(1.0))
        mag = jnp.exp(-r) * sponge
        cr = mag * jnp.cos(ph)
        ci = mag * jnp.sin(ph)
        sc = jnp.sqrt(-expm1(-2.0 * r))
        coef_ref[0, i] = cr
        coef_ref[1, i] = ci
        coef_ref[2, i] = sc
        npr = cr * pr - ci * pi
        npi = cr * pi + ci * pr
        nxr, nxi = [], []
        for e in range(ex):
            fr = station(fbuf.at[e], i, fields, stations)
            fi = station(fbuf.at[ex + e], i, fields, stations)
            nxr.append(cr * xr[e] - ci * xi[e] + sc * fr)
            nxi.append(cr * xi[e] + ci * xr[e] + sc * fi)
        return npr, npi, tuple(nxr), tuple(nxi)

    shape = (fields, wall)
    one = jnp.ones(shape, jnp.float32)
    zero = jnp.zeros(shape, jnp.float32)
    init = (one, zero, (zero,) * ex, (zero,) * ex)
    pr, pi, xr, xi = lax.fori_loop(0, stations, step, init, unroll=4)

    values = [(xr[e], xi[e]) for e in range(ex)] + [(pr, pi)]
    for j, pair in enumerate(values):
        for c in range(2):
            tmp[...] = pair[c]
            for f in range(fields):
                for q in range(chunks):
                    pack[c, j, pl.ds(f * chunks + q, 1), :] = tmp[
                        pl.ds(f, 1), pl.ds(q * LANES, LANES)
                    ]

    pl.semaphore_wait(barrier, len(partners))

    def put(buf, n, i, value):
        rows = pl.ds(i, fields, stride=stations)
        for q in range(chunks):
            buf[n, q, rows, :] = value[:, q * LANES:(q + 1) * LANES]

    def local_march(lo, hi, carry):
        def step(i, carry):
            pr, pi, xr, xi = carry
            cr = coef_ref[0, i]
            ci = coef_ref[1, i]
            sc = coef_ref[2, i]
            npr = cr * pr - ci * pi
            npi = cr * pi + ci * pr
            put(gbuf, 0, i, npr)
            put(gbuf, 1, i, npi)
            nxr, nxi = [], []
            for e in range(ex):
                fr = station(fbuf.at[e], i, fields, stations)
                fi = station(fbuf.at[ex + e], i, fields, stations)
                r = cr * xr[e] - ci * xi[e] + sc * fr
                m = cr * xi[e] + ci * xr[e] + sc * fi
                put(qbuf, e, i, r)
                put(qbuf, ex + e, i, m)
                nxr.append(r)
                nxi.append(m)
            return npr, npi, tuple(nxr), tuple(nxi)

        return lax.fori_loop(lo, hi, step, carry, unroll=4)

    def load(ref):
        return [(ref[0, j], ref[1, j]) for j in range(ex + 1)]

    def compose(earlier, later):
        ar, ai = later[ex]
        out = []
        for j in range(ex + 1):
            br, bi = earlier[j]
            nr = ar * br - ai * bi
            ni = ar * bi + ai * br
            if j < ex:
                nr = nr + later[j][0]
                ni = ni + later[j][1]
            out.append((nr, ni))
        return out

    held = None
    for k in range(len(rounds)):
        mine = [i for i, (r, _) in enumerate(slots) if r == k]
        src = pack if k == 0 else cur.at[k]
        copies = []
        for i in mine:
            copy = pltpu.make_async_remote_copy(
                src_ref=src,
                dst_ref=recv.at[i],
                send_sem=send_sem.at[i],
                recv_sem=recv_sem.at[i],
                device_id=device(slots[i][1]),
                device_id_type=MESH,
            )
            copy.start()
            copies.append(copy)
        if k == 0:
            marched = local_march(0, stations // 2, init)
        if k == 1:
            local_march(stations // 2, stations, marched)
        for n, (i, copy) in enumerate(zip(mine, copies)):
            copy.wait()
            arrived = load(recv.at[i])
            held = arrived if (k == 0 and n == 0) else compose(arrived, held)
        if k + 1 < len(rounds):
            dst = cur.at[k + 1]
            for j, (nr, ni) in enumerate(held):
                dst[0, j] = nr
                dst[1, j] = ni
            held = load(dst)

    gr, gi = held[ex]
    denom_re = 1.0 - gr
    denom_im = -gi
    size = denom_re * denom_re + denom_im * denom_im
    ent = cur.at[0]
    for j in range(ex):
        br, bi = held[j]
        ent[0, j] = (br * denom_re + bi * denom_im) / size
        ent[1, j] = (bi * denom_re - br * denom_im) / size
    for c in range(2):
        for e in range(ex):
            for f in range(fields):
                for q in range(chunks):
                    x0_ref[c, e, pl.ds(f, 1), pl.ds(q * LANES, LANES)] = ent[
                        c, e, pl.ds(f * chunks + q, 1), :
                    ]

    copies = []
    for e in range(ex):
        for q in range(chunks):
            lanes = pl.ds(q * LANES, LANES)
            for f in range(fields):
                rows = pl.ds(f * stations, stations)
                xr = x0_ref[0, e, pl.ds(f, 1), lanes]
                xi = x0_ref[1, e, pl.ds(f, 1), lanes]
                gr = gbuf[0, q, rows, :]
                gi = gbuf[1, q, rows, :]
                qbuf[e, q, rows, :] = qbuf[e, q, rows, :] + (gr * xr - gi * xi)
                qbuf[ex + e, q, rows, :] = qbuf[ex + e, q, rows, :] + (gr * xi + gi * xr)
            for n in (e, ex + e):
                copy = pltpu.make_async_copy(
                    qbuf.at[n, q], out_hbm.at[n, :, lanes], out_sem.at[n * chunks + q]
                )
                copy.start()
                copies.append(copy)
    for copy in copies:
        copy.wait()


def local(rate, phase, forcing):
    stations, fields, wall = rate.shape
    two, ex = forcing.shape[:2]
    count = lax.axis_size(AXES)
    subs = lax.axis_size("sub")
    rate_t = jnp.transpose(rate, (1, 0, 2)).reshape(fields * stations, wall)
    phase_t = jnp.transpose(phase, (1, 0, 2)).reshape(fields * stations, wall)
    forcing_t = jnp.transpose(forcing, (0, 1, 3, 2, 4)).reshape(
        two * ex, fields * stations, wall
    )
    n_slots = len(slots_of(count))
    n_rounds = len(rounds_of(count))
    packed = (2, ex + 1, fields * wall // LANES, LANES)
    vmem = pl.BlockSpec(memory_space=pltpu.VMEM)
    hbm = pl.BlockSpec(memory_space=pl.ANY)
    chunks = wall // LANES
    slab = (fields * stations, LANES)
    fbuf = pltpu.VMEM((two * ex, chunks) + slab, jnp.float32)
    out_t = pl.pallas_call(
        functools.partial(resolvent_kernel, count, subs),
        out_shape=jax.ShapeDtypeStruct(forcing_t.shape, jnp.float32),
        in_specs=[hbm] * 3,
        out_specs=hbm,
        scratch_shapes=[
            pltpu.VMEM((chunks,) + slab, jnp.float32),
            pltpu.VMEM((chunks,) + slab, jnp.float32),
            fbuf,
            pltpu.SemaphoreType.DMA(((2 + two * ex) * chunks,)),
            pltpu.VMEM((3, stations, fields, wall), jnp.float32),
            pltpu.VMEM((2, ex, fields, wall), jnp.float32),
            fbuf,
            pltpu.VMEM((2, chunks) + slab, jnp.float32),
            pltpu.SemaphoreType.DMA((two * ex * chunks,)),
            pltpu.VMEM((fields, wall), jnp.float32),
            pltpu.VMEM(packed, jnp.float32),
            pltpu.VMEM((n_slots,) + packed, jnp.float32),
            pltpu.VMEM((n_rounds,) + packed, jnp.float32),
            pltpu.SemaphoreType.DMA((n_slots,)),
            pltpu.SemaphoreType.DMA((n_slots,)),
        ],
        compiler_params=pltpu.CompilerParams(collective_id=0, has_side_effects=True),
    )(rate_t, phase_t, forcing_t)
    return jnp.transpose(out_t.reshape(two, ex, fields, stations, wall), (0, 1, 3, 2, 4))


def solution(mesh):
    count = mesh.shape["loop"] * mesh.shape["sub"]
    assert count & (count - 1) == 0
    placed = (
        P(AXES, None, None),
        P(AXES, None, None),
        P(None, None, AXES, None, None),
    )
    return jax.shard_map(
        local,
        mesh=mesh,
        in_specs=placed,
        out_specs=P(None, None, AXES, None, None),
        check_vma=False,
    )
```

```python
import functools

import jax
import jax.numpy as jnp
from jax import lax
from jax.experimental import pallas as pl
from jax.experimental.pallas import tpu as pltpu
from jax.sharding import PartitionSpec as P

fringe_total = 0.7
FRINGE_STATIONS = 32
AXES = ("loop", "sub")
MESH = pl.DeviceIdType.MESH
LANES = 128


def rounds_of(count):
    out, reach = [], 1
    while reach < count:
        fan = 4 if count % (reach * 4) == 0 else 2
        out.append((reach, fan))
        reach *= fan
    return out


def slots_of(count):
    slots = []
    for k, (stride, fan) in enumerate(rounds_of(count)):
        for j in range(1, fan + (1 if k == 0 else 0)):
            slots.append((k, j * stride))
    return slots


def expm1(x):
    u = jnp.exp(x)
    return jnp.where(u == 1.0, x, (u - 1.0) * x / jnp.log(u))


def fetch(srcs, bufs, sems):
    copies = []
    for n, (src, buf) in enumerate(zip(srcs, bufs)):
        for q in range(buf.shape[0]):
            copy = pltpu.make_async_copy(
                src.at[:, pl.ds(q * LANES, LANES)], buf.at[q], sems.at[n * buf.shape[0] + q]
            )
            copy.start()
            copies.append(copy)
    return copies


def station(buf, i, fields, stations):
    rows = pl.ds(i, fields, stride=stations)
    return jnp.concatenate([buf[q, rows, :] for q in range(buf.shape[0])], axis=1)


def resolvent_kernel(count, subs, rate_hbm, phase_hbm, f_hbm, out_hbm,
                     rbuf, pbuf, fbuf, in_sem, coef_ref, x0_ref, qbuf, gbuf, out_sem,
                     tmp, pack, recv, cur, send_sem, recv_sem):
    ex = x0_ref.shape[1]
    stations, fields, wall = coef_ref.shape[1:]
    chunks = wall // LANES
    copies = fetch(
        [rate_hbm, phase_hbm] + [f_hbm.at[n] for n in range(2 * ex)],
        [rbuf, pbuf] + [fbuf.at[n] for n in range(2 * ex)],
        in_sem,
    )
    me = lax.axis_index("loop") * subs + lax.axis_index("sub")
    rounds = rounds_of(count)
    slots = slots_of(count)

    def device(offset):
        t = lax.rem(me + offset + count, count)
        return (t // subs, lax.rem(t, subs))

    partners = sorted({o % count for _, o in slots} | {(-o) % count for _, o in slots})
    barrier = pltpu.get_barrier_semaphore()
    for p in partners:
        pl.semaphore_signal(barrier, inc=1, device_id=device(p), device_id_type=MESH)

    first_fringe = count * stations - FRINGE_STATIONS
    damp = jnp.float32(fringe_total ** (1.0 / FRINGE_STATIONS))
    for copy in copies:
        copy.wait()

    def step(i, carry):
        pr, pi, xr, xi = carry
        r = station(rbuf, i, fields, stations)
        ph = station(pbuf, i, fields, stations)
        sponge = jnp.where(me * stations + i >= first_fringe, damp, jnp.float32(1.0))
        mag = jnp.exp(-r) * sponge
        cr = mag * jnp.cos(ph)
        ci = mag * jnp.sin(ph)
        sc = jnp.sqrt(-expm1(-2.0 * r))
        coef_ref[0, i] = cr
        coef_ref[1, i] = ci
        coef_ref[2, i] = sc
        npr = cr * pr - ci * pi
        npi = cr * pi + ci * pr
        nxr, nxi = [], []
        for e in range(ex):
            fr = station(fbuf.at[e], i, fields, stations)
            fi = station(fbuf.at[ex + e], i, fields, stations)
            nxr.append(cr * xr[e] - ci * xi[e] + sc * fr)
            nxi.append(cr * xi[e] + ci * xr[e] + sc * fi)
        return npr, npi, tuple(nxr), tuple(nxi)

    shape = (fields, wall)
    one = jnp.ones(shape, jnp.float32)
    zero = jnp.zeros(shape, jnp.float32)
    init = (one, zero, (zero,) * ex, (zero,) * ex)
    pr, pi, xr, xi = lax.fori_loop(0, stations, step, init, unroll=4)

    values = [(xr[e], xi[e]) for e in range(ex)] + [(pr, pi)]
    for j, pair in enumerate(values):
        for c in range(2):
            tmp[...] = pair[c]
            for f in range(fields):
                for q in range(chunks):
                    pack[c, j, pl.ds(f * chunks + q, 1), :] = tmp[
                        pl.ds(f, 1), pl.ds(q * LANES, LANES)
                    ]

    pl.semaphore_wait(barrier, len(partners))

    def put(buf, n, i, value):
        rows = pl.ds(i, fields, stride=stations)
        for q in range(chunks):
            buf[n, q, rows, :] = value[:, q * LANES:(q + 1) * LANES]

    def local_march(lo, hi, carry):
        def step(i, carry):
            pr, pi, xr, xi = carry
            cr = coef_ref[0, i]
            ci = coef_ref[1, i]
            sc = coef_ref[2, i]
            npr = cr * pr - ci * pi
            npi = cr * pi + ci * pr
            put(gbuf, 0, i, npr)
            put(gbuf, 1, i, npi)
            nxr, nxi = [], []
            for e in range(ex):
                fr = station(fbuf.at[e], i, fields, stations)
                fi = station(fbuf.at[ex + e], i, fields, stations)
                r = cr * xr[e] - ci * xi[e] + sc * fr
                m = cr * xi[e] + ci * xr[e] + sc * fi
                put(qbuf, e, i, r)
                put(qbuf, ex + e, i, m)
                nxr.append(r)
                nxi.append(m)
            return npr, npi, tuple(nxr), tuple(nxi)

        return lax.fori_loop(lo, hi, step, carry, unroll=4)

    def load(ref):
        return [(ref[0, j], ref[1, j]) for j in range(ex + 1)]

    def compose(earlier, later):
        ar, ai = later[ex]
        out = []
        for j in range(ex + 1):
            br, bi = earlier[j]
            nr = ar * br - ai * bi
            ni = ar * bi + ai * br
            if j < ex:
                nr = nr + later[j][0]
                ni = ni + later[j][1]
            out.append((nr, ni))
        return out

    held = None
    for k in range(len(rounds)):
        mine = [i for i, (r, _) in enumerate(slots) if r == k]
        src = pack if k == 0 else cur.at[k]
        copies = []
        for i in mine:
            copy = pltpu.make_async_remote_copy(
                src_ref=src,
                dst_ref=recv.at[i],
                send_sem=send_sem.at[i],
                recv_sem=recv_sem.at[i],
                device_id=device(slots[i][1]),
                device_id_type=MESH,
            )
            copy.start()
            copies.append(copy)
        if k == 0:
            marched = local_march(0, stations // 2, init)
        if k == 1:
            local_march(stations // 2, stations, marched)
        for n, (i, copy) in enumerate(zip(mine, copies)):
            copy.wait()
            arrived = load(recv.at[i])
            held = arrived if (k == 0 and n == 0) else compose(arrived, held)
        if k + 1 < len(rounds):
            dst = cur.at[k + 1]
            for j, (nr, ni) in enumerate(held):
                dst[0, j] = nr
                dst[1, j] = ni
            held = load(dst)

    gr, gi = held[ex]
    denom_re = 1.0 - gr
    denom_im = -gi
    size = denom_re * denom_re + denom_im * denom_im
    ent = cur.at[0]
    for j in range(ex):
        br, bi = held[j]
        ent[0, j] = (br * denom_re + bi * denom_im) / size
        ent[1, j] = (bi * denom_re - br * denom_im) / size

    copies = []
    for e in range(ex):
        for q in range(chunks):
            lanes = pl.ds(q * LANES, LANES)
            for f in range(fields):
                rows = pl.ds(f * stations, stations)
                xr = ent[0, e, pl.ds(f * chunks + q, 1), :]
                xi = ent[1, e, pl.ds(f * chunks + q, 1), :]
                gr = gbuf[0, q, rows, :]
                gi = gbuf[1, q, rows, :]
                qbuf[e, q, rows, :] = qbuf[e, q, rows, :] + (gr * xr - gi * xi)
                qbuf[ex + e, q, rows, :] = qbuf[ex + e, q, rows, :] + (gr * xi + gi * xr)
            for n in (e, ex + e):
                copy = pltpu.make_async_copy(
                    qbuf.at[n, q], out_hbm.at[n, :, lanes], out_sem.at[n * chunks + q]
                )
                copy.start()
                copies.append(copy)
    for copy in copies:
        copy.wait()


def local(rate, phase, forcing):
    stations, fields, wall = rate.shape
    two, ex = forcing.shape[:2]
    count = lax.axis_size(AXES)
    subs = lax.axis_size("sub")
    rate_t = jnp.transpose(rate, (1, 0, 2)).reshape(fields * stations, wall)
    phase_t = jnp.transpose(phase, (1, 0, 2)).reshape(fields * stations, wall)
    forcing_t = jnp.transpose(forcing, (0, 1, 3, 2, 4)).reshape(
        two * ex, fields * stations, wall
    )
    n_slots = len(slots_of(count))
    n_rounds = len(rounds_of(count))
    packed = (2, ex + 1, fields * wall // LANES, LANES)
    vmem = pl.BlockSpec(memory_space=pltpu.VMEM)
    hbm = pl.BlockSpec(memory_space=pl.ANY)
    chunks = wall // LANES
    slab = (fields * stations, LANES)
    fbuf = pltpu.VMEM((two * ex, chunks) + slab, jnp.float32)
    out_t = pl.pallas_call(
        functools.partial(resolvent_kernel, count, subs),
        out_shape=jax.ShapeDtypeStruct(forcing_t.shape, jnp.float32),
        in_specs=[hbm] * 3,
        out_specs=hbm,
        scratch_shapes=[
            pltpu.VMEM((chunks,) + slab, jnp.float32),
            pltpu.VMEM((chunks,) + slab, jnp.float32),
            fbuf,
            pltpu.SemaphoreType.DMA(((2 + two * ex) * chunks,)),
            pltpu.VMEM((3, stations, fields, wall), jnp.float32),
            pltpu.VMEM((2, ex, fields, wall), jnp.float32),
            fbuf,
            pltpu.VMEM((2, chunks) + slab, jnp.float32),
            pltpu.SemaphoreType.DMA((two * ex * chunks,)),
            pltpu.VMEM((fields, wall), jnp.float32),
            pltpu.VMEM(packed, jnp.float32),
            pltpu.VMEM((n_slots,) + packed, jnp.float32),
            pltpu.VMEM((n_rounds,) + packed, jnp.float32),
            pltpu.SemaphoreType.DMA((n_slots,)),
            pltpu.SemaphoreType.DMA((n_slots,)),
        ],
        compiler_params=pltpu.CompilerParams(collective_id=0, has_side_effects=True),
    )(rate_t, phase_t, forcing_t)
    return jnp.transpose(out_t.reshape(two, ex, fields, stations, wall), (0, 1, 3, 2, 4))


def solution(mesh):
    count = mesh.shape["loop"] * mesh.shape["sub"]
    assert count & (count - 1) == 0
    placed = (
        P(AXES, None, None),
        P(AXES, None, None),
        P(None, None, AXES, None, None),
    )
    return jax.shard_map(
        local,
        mesh=mesh,
        in_specs=placed,
        out_specs=P(None, None, AXES, None, None),
        check_vma=False,
    )
```
